1024 devices in a mesh: seq: 16 (over x, y), row: 8 (over z_hi, core), col: 8 (over z_lo).
Axes of the slice: x: 4, y: 4, z: 32 (z_hi: 4, z_lo: 8; z = z_hi * 8 + z_lo), core: 2. Of those that a mesh axis runs over, the one named last changes fastest.
Arguments:
- query_rows: bfloat16 [2048, 16384], P('seq', ('row', 'col')), may hold values from -9.5625 to 9.5625
- key_rows: bfloat16 [2048, 16384], P('seq', ('row', 'col')), may hold values from -16 to 16
- value_rows: bfloat16 [2048, 16384], P('seq', ('row', 'col')), may hold values from -6 to 6
- out_grad: bfloat16 [2048, 16384], P('seq', ('row', 'col')), may hold values from -6 to 6
- mix_pre: bfloat16 [128, 128], replicated, may hold values from -0.3 to 1.3
- mix_post: bfloat16 [128, 128], replicated, may hold values from -0.3 to 1.3
- block_order: int32 [16], replicated, may hold values from 0 to 15, each once
Outputs:
- attention_out: bfloat16 [2048, 16384], P('seq', ('row', 'col'))
- grad_query: bfloat16 [2048, 16384], P('seq', ('row', 'col'))
- grad_key: bfloat16 [2048, 16384], P('seq', ('row', 'col'))
- grad_value: bfloat16 [2048, 16384], P('seq', ('row', 'col'))
The draws below stay inside these ranges and needn't reach their ends.
Inputs may be any that keep to these rules, and one draw needn't show every extreme that they name: block_order holds every number below 16 once.
All inputs are finite; a program needn't handle non-finite values.
Results may differ from the reference program's by a relative error of at most 0.012.
Values may be sent and summed in bfloat16 or wider, within the bound.
No kernel may reach another device: no remote copies, remote signals or barrier semaphores. Data moves between devices by JAX's collectives and lax.ppermute only.
A program may use at most 32 MiB of HBM per device.

```python
import jax
import jax.numpy as jnp
from jax import lax

H = 128
DH = 128
QB = 128
BLOCKS = 16
SEQ = 2048


def mixing(seed_key):
    noise = jnp.clip(jax.random.normal(seed_key, (H, H), jnp.float32), -4.0, 4.0)
    table = jnp.eye(H, dtype=jnp.float32) + 0.5 * noise / jnp.sqrt(jnp.float32(H))
    return table.astype(jnp.bfloat16)


def draw_mix_pre(key, part):
    return mixing(jax.random.fold_in(key, 11))


def draw_mix_post(key, part):
    return mixing(jax.random.fold_in(key, 23))


def draw_key_rows(key, part):
    scale_key = jax.random.fold_in(key, 31)
    entry_key = jax.random.fold_in(key, 37)
    row_scale = jnp.exp(jax.random.uniform(scale_key, (SEQ, 1), jnp.float32, jnp.log(0.5), jnp.log(1.0)))
    entries = jnp.clip(jax.random.normal(entry_key, (SEQ, H * DH), jnp.float32), -4.0, 4.0)
    return (entries * row_scale).astype(jnp.bfloat16)


def block_levels(stream_key, shape, shards, smallest, high):
    def one(dim, shards_of):
        draws = jax.random.uniform(jax.random.fold_in(jax.random.fold_in(stream_key, 6), dim), (shards_of,), jnp.float32, smallest / len(shards), high / len(shards))
        return jnp.repeat(jnp.exp(draws), shape[dim] // shards_of).reshape((-1,) + (1,) * (len(shape) - dim - 1))

    gain = one(*shards[0])
    for cut in shards[1:]:
        gain = gain * one(*cut)
    return gain


def gaussian(rng, extent, scale, reach, shards=(), kind=jnp.bfloat16):
    values = jax.random.normal(rng, extent, jnp.float32) * scale
    if len(shards) > 0:
        values = block_levels(rng, extent, shards, -0.22, 0.18) * values
    return jnp.clip(values, min=-reach, max=reach).astype(kind)


def setup_inputs(seed: int = 0) -> dict:
    key_of = jax.random.split(jax.random.key(seed), 8)
    query_rows = gaussian(key_of[0], (SEQ, H * DH), 1.6, 9.5625, ((0, 16), (1, 64)))
    key_rows = draw_key_rows(jax.random.fold_in(key_of[7], 71), 0)
    value_rows = gaussian(key_of[2], (SEQ, H * DH), 1.0, 6.0, ((0, 16), (1, 64)))
    out_grad = gaussian(key_of[3], (SEQ, H * DH), 1.0, 6.0, ((0, 16), (1, 64)))
    mix_pre = draw_mix_pre(jax.random.fold_in(key_of[7], 71), 0)
    mix_post = draw_mix_post(jax.random.fold_in(key_of[7], 71), 0)
    block_order = jax.random.permutation(key_of[6], BLOCKS).astype(jnp.int32)
    return {"query_rows": query_rows, "key_rows": key_rows, "value_rows": value_rows, "out_grad": out_grad, "mix_pre": mix_pre, "mix_post": mix_post, "block_order": block_order}


logit_cap = 10.0


def rounded(values):
    return lax.optimization_barrier(values.astype(jnp.bfloat16)).astype(jnp.float32)


def reference(query_rows, key_rows, value_rows, out_grad, mix_pre, mix_post, block_order):
    scaling = DH ** -0.5
    query_all = query_rows.astype(jnp.float32).reshape(SEQ, H, DH)
    key_all = key_rows.astype(jnp.float32).reshape(SEQ, H, DH)
    value_all = value_rows.astype(jnp.float32).reshape(SEQ, H, DH)
    upstream = out_grad.astype(jnp.float32).reshape(SEQ, H, DH)
    pre_mix = mix_pre.astype(jnp.float32)
    post_mix = mix_post.astype(jnp.float32)
    place = (jnp.repeat(block_order, QB) * QB + jnp.tile(jnp.arange(QB, dtype=jnp.int32), BLOCKS)).astype(jnp.int32)

    def one_block(sums_pair, number):
        key_sum, value_sum = sums_pair
        first_row = (number * QB).astype(jnp.int32)
        query_blk = lax.dynamic_slice_in_dim(query_all, first_row, QB, 0)
        grad_blk = lax.dynamic_slice_in_dim(upstream, first_row, QB, 0)
        query_place = lax.dynamic_slice_in_dim(place, first_row, QB, 0)
        scores = rounded(jnp.einsum("qhd,khd->hqk", query_blk, key_all) * scaling)
        mixed = jnp.einsum("gh,hqk->gqk", pre_mix, scores)
        capped = logit_cap * jnp.tanh(mixed / logit_cap)
        allowed = place[None, None, :] <= query_place[None, :, None]
        weights = jnp.where(allowed, jnp.exp(capped), jnp.float32(0.0))
        probs = weights / jnp.sum(weights, axis=2, keepdims=True)
        probs16 = rounded(probs)
        post_mixed = rounded(jnp.einsum("gh,hqk->gqk", post_mix, probs16))
        attended = jnp.einsum("hqk,khd->qhd", post_mixed, value_all).astype(jnp.bfloat16)
        grad_post = rounded(jnp.einsum("qhd,khd->hqk", grad_blk, value_all))
        grad_probs = jnp.einsum("gh,gqk->hqk", post_mix, grad_post)
        rowdot = jnp.sum(probs * grad_probs, axis=2, keepdims=True)
        grad_capped = probs * (grad_probs - rowdot)
        grad_mixed = rounded(grad_capped * (1.0 - (capped / logit_cap) ** 2))
        grad_scores = rounded(scaling * jnp.einsum("gh,gqk->hqk", pre_mix, grad_mixed))
        grad_rows = jnp.einsum("hqk,khd->qhd", grad_scores, key_all).astype(jnp.bfloat16)
        key_part = rounded(jnp.einsum("hqk,qhd->khd", grad_scores, query_blk))
        value_part = rounded(jnp.einsum("hqk,qhd->khd", post_mixed, grad_blk))
        return (key_sum + key_part, value_sum + value_part), (attended, grad_rows)

    start_sums = (jnp.zeros((SEQ, H, DH), jnp.float32), jnp.zeros((SEQ, H, DH), jnp.float32))
    (key_sum, value_sum), (attended, grad_rows) = lax.scan(one_block, start_sums, jnp.arange(BLOCKS, dtype=jnp.int32))
    attention_out = attended.reshape(SEQ, H * DH)
    grad_query = grad_rows.reshape(SEQ, H * DH)
    grad_key = key_sum.astype(jnp.bfloat16).reshape(SEQ, H * DH)
    grad_value = value_sum.astype(jnp.bfloat16).reshape(SEQ, H * DH)
    return (attention_out, grad_query, grad_key, grad_value)
```

```python
import jax
import jax.numpy as jnp
from jax import lax
from jax.sharding import PartitionSpec as P

DH = 128


logit_cap = 10.0

HEAD_AXES = ("row", "col")


def body(query_rows, key_rows, value_rows, out_grad, mix_pre, mix_post, block_order):
    blocks = lax.axis_size("seq")
    owners = lax.axis_size("row") * lax.axis_size("col")
    rows, width = query_rows.shape
    heads_local = width // DH
    heads_all = mix_pre.shape[0]
    scaling = DH ** (-0.5)
    strip = rows // blocks
    half = blocks // 2
    span = (blocks + 1) * rows
    seq_len = blocks * rows
    seq_index = lax.axis_index("seq")

    key_value = jnp.concatenate([key_rows, value_rows], axis=1)
    query_grad = jnp.concatenate([query_rows, out_grad], axis=1).reshape(blocks, strip, 2 * width)
    sent = jnp.concatenate(
        [jnp.broadcast_to(key_value[None], (blocks, rows, 2 * width)), query_grad], axis=1
    )
    received = lax.all_to_all(sent, "seq", split_axis=0, concat_axis=0, tiled=True)
    numbers = jnp.arange(blocks, dtype=jnp.int32)
    stored_at = jnp.sum(
        jnp.where(block_order[None, :] == numbers[:, None], numbers[None, :], 0), axis=1
    )
    by_place = jnp.take(received, stored_at, axis=0)
    key_value_all = by_place[:, :rows].reshape(seq_len, 2, heads_local, DH)
    query_grad_all = by_place[:, rows:].reshape(rows, 2, heads_local, DH)
    key_heads, value_heads = key_value_all[:, 0], key_value_all[:, 1]
    query_heads, upstream = query_grad_all[:, 0], query_grad_all[:, 1]

    def pack(dense):
        view = dense.reshape(heads_local, blocks, strip, seq_len)
        parts = []
        for c in range(half):
            near = view[:, c, :, : rows * (c + 1)]
            far = view[:, blocks - 1 - c, :, : rows * (blocks - c)]
            parts.append(jnp.concatenate([near, far], axis=2))
        return jnp.concatenate(parts, axis=1)

    def unpack(packed):
        view = packed.reshape(-1, half, strip, span)
        parts = []
        for p in range(blocks):
            if p < half:
                piece = view[:, p, :, : rows * (p + 1)]
            else:
                piece = view[:, blocks - 1 - p, :, rows * (blocks - p) :]
            parts.append(jnp.pad(piece, ((0, 0), (0, 0), (0, seq_len - rows * (p + 1)))))
        return jnp.concatenate(parts, axis=1)

    scores = (
        jnp.einsum("qhd,khd->hqk", query_heads, key_heads, preferred_element_type=jnp.float32)
        * scaling
    ).astype(jnp.bfloat16)
    grad_post = jnp.einsum(
        "qhd,khd->hqk", upstream, value_heads, preferred_element_type=jnp.float32
    ).astype(jnp.bfloat16)
    outgoing = jnp.concatenate([pack(scores), pack(grad_post)], axis=0)
    incoming = lax.all_to_all(outgoing, HEAD_AXES, split_axis=1, concat_axis=1, tiled=True)
    incoming = incoming.reshape(2, heads_all, span)

    def reorder(mix):
        view = mix.reshape(owners, heads_local, owners, heads_local)
        return view.transpose(1, 0, 3, 2).reshape(heads_all, heads_all)

    pre, post = reorder(mix_pre), reorder(mix_post)
    own = lax.axis_index(HEAD_AXES)
    pair, line = own // strip, own % strip
    bound = rows * (pair + 1)
    lane = lax.broadcasted_iota(jnp.int32, (1, span), 1)
    is_near = lane < bound
    key_place = jnp.where(is_near, lane, lane - bound)
    query_place = (
        jnp.where(is_near, pair, blocks - 1 - pair) * rows + seq_index * strip + line
    )
    allowed = key_place <= query_place

    def row_sum(values):
        near = jnp.sum(jnp.where(is_near, values, 0.0), axis=1, keepdims=True)
        far = jnp.sum(jnp.where(is_near, 0.0, values), axis=1, keepdims=True)
        return near, far

    mixed = jnp.dot(pre, incoming[0], preferred_element_type=jnp.float32)
    squashed = jnp.tanh(mixed / logit_cap)
    weights = jnp.where(allowed, jnp.exp(logit_cap * squashed), 0.0)
    near_total, far_total = row_sum(weights)
    probs = weights * jnp.where(is_near, 1.0 / near_total, 1.0 / far_total)
    post_mixed = jnp.dot(
        post, probs.astype(jnp.bfloat16), preferred_element_type=jnp.float32
    ).astype(jnp.bfloat16)
    grad_probs = jnp.einsum("gh,gk->hk", post, incoming[1], preferred_element_type=jnp.float32)
    near_dot, far_dot = row_sum(probs * grad_probs)
    grad_capped = probs * (grad_probs - jnp.where(is_near, near_dot, far_dot))
    grad_mixed = (grad_capped * (1.0 - squashed * squashed)).astype(jnp.bfloat16)
    grad_scores = (
        scaling * jnp.einsum("gh,gk->hk", pre, grad_mixed, preferred_element_type=jnp.float32)
    ).astype(jnp.bfloat16)

    outgoing = jnp.concatenate([post_mixed, grad_scores], axis=0).reshape(
        2 * heads_local, owners, span
    )
    incoming = lax.all_to_all(outgoing, HEAD_AXES, split_axis=1, concat_axis=1, tiled=True)
    post_dense = unpack(incoming[:heads_local])
    score_dense = unpack(incoming[heads_local:])

    def rounded(spec, left, right):
        return jnp.einsum(spec, left, right, preferred_element_type=jnp.float32).astype(
            jnp.bfloat16
        )

    attended = rounded("hqk,khd->qhd", post_dense, value_heads)
    grad_query = rounded("hqk,khd->qhd", score_dense, key_heads)
    key_term = rounded("hqk,qhd->khd", score_dense, query_heads)
    value_term = rounded("hqk,qhd->khd", post_dense, upstream)
    terms = jnp.stack([key_term, value_term], axis=1).reshape(blocks, rows, 2 * width)
    results = jnp.stack([attended, grad_query], axis=1).reshape(blocks, strip, 2 * width)
    sent = jnp.take(jnp.concatenate([terms, results], axis=1), block_order, axis=0)
    received = lax.all_to_all(sent, "seq", split_axis=0, concat_axis=0, tiled=True)
    summed = jnp.sum(received[:, :rows].astype(jnp.float32), axis=0).astype(jnp.bfloat16)
    results = received[:, rows:].reshape(rows, 2 * width)
    return (results[:, :width], results[:, width:], summed[:, :width], summed[:, width:])


def solution(mesh):
    spread = P("seq", HEAD_AXES)
    return jax.shard_map(
        body,
        mesh=mesh,
        in_specs=(spread, spread, spread, spread, P(), P(), P()),
        out_specs=(spread, spread, spread, spread),
        check_vma=False,
    )
```

```python
import functools

import jax
import jax.numpy as jnp
from jax import lax
from jax.experimental import pallas as pl
from jax.experimental.pallas import tpu as pltpu
from jax.sharding import PartitionSpec as P

DH = 128


logit_cap = 10.0

HEAD_AXES = ("row", "col")
KINDS = 4
CHUNK = 4
INTERP = False


def place_of(p, b, half, blocks, rows):
    return (b if p < half else blocks - p + b) * rows


def pair_of(p, half, blocks):
    return p if p < half else blocks - 1 - p


def send_kernel(query_ref, key_ref, value_ref, grad_ref, out_ref, *, blocks, rows, strip, width):
    for s in range(blocks):
        out_ref[s, :rows, :width] = key_ref[...]
        out_ref[s, :rows, width:] = value_ref[...]
        out_ref[s, rows:, :width] = query_ref[s * strip : (s + 1) * strip, :]
        out_ref[s, rows:, width:] = grad_ref[s * strip : (s + 1) * strip, :]


def score_kernel(
    order_ref, received_ref, out_ref, key_value_ref, spread_ref, lines_ref, *, blocks, rows, strip, scaling
):
    half = blocks // 2
    group = KINDS * strip
    for p in range(blocks):
        source = order_ref[p]
        key_value_ref[p * rows : (p + 1) * rows, :] = received_ref[source, :rows, :]
        lines_ref[p * strip : (p + 1) * strip, :] = received_ref[source, rows:, :].astype(jnp.float32)
    total = blocks * group
    row = lax.broadcasted_iota(jnp.int32, (total, blocks * strip), 0)
    line = lax.broadcasted_iota(jnp.int32, (total, blocks * strip), 1)
    repeat = jnp.where(row // KINDS == line, 1.0, 0.0).astype(jnp.bfloat16)
    repeated = jnp.dot(
        repeat, lines_ref[...].astype(jnp.bfloat16), preferred_element_type=jnp.float32
    )
    row = lax.broadcasted_iota(jnp.int32, (total, KINDS * DH), 0)
    column = lax.broadcasted_iota(jnp.int32, (total, KINDS * DH), 1)
    spread_ref[...] = jnp.where(row % KINDS == column // DH, repeated, 0.0).astype(jnp.bfloat16)
    for j in range(blocks // CHUNK):
        first = j * CHUNK
        keys = key_value_ref[first * rows : (first + CHUNK) * rows, :]
        scores = lax.dot_general(
            spread_ref[first * group :, :],
            keys,
            (((1,), (1,)), ((), ())),
            preferred_element_type=jnp.float32,
        )
        kind = lax.broadcasted_iota(jnp.int32, scores.shape, 0) % KINDS
        scores = jnp.where(kind < KINDS // 2, scores * scaling, scores).astype(jnp.bfloat16)
        for p in range(first, blocks):
            count = min(p - first + 1, CHUNK)
            c = pair_of(p, half, blocks)
            lane = place_of(p, first, half, blocks, rows)
            out_ref[c * group : (c + 1) * group, lane : lane + count * rows] = scores[
                (p - first) * group : (p - first + 1) * group, : count * rows
            ]


def mix_kernel(
    where_ref, incoming_ref, before_ref, after_ref, out_ref, squashed_ref, weight_ref, grad_ref, both_ref,
    *, blocks, rows, heads, scaling
):
    pair, offset = where_ref[0], where_ref[1]
    zero = jnp.zeros((heads, rows), jnp.float32)
    near_total, far_total, near_dot, far_dot = zero, zero, zero, zero
    lane = lax.broadcasted_iota(jnp.int32, (heads, rows), 1)
    tiles = blocks + 1
    for j in range(tiles):
        cut = slice(j * rows, (j + 1) * rows)
        mixed = jnp.dot(
            before_ref[...], incoming_ref[:, cut], preferred_element_type=jnp.float32
        )
        is_near = j <= pair
        start = (j - jnp.where(is_near, 0, pair + 1)) * rows
        limit = jnp.where(is_near, pair, blocks - 1 - pair) * rows + offset - start
        squashed = jnp.tanh(mixed[:heads] / logit_cap)
        weights = jnp.where(lane <= limit, jnp.exp(logit_cap * squashed), 0.0)
        grad_probs = mixed[heads:]
        squashed_ref[:, cut] = squashed
        weight_ref[:, cut] = weights
        grad_ref[:, cut] = grad_probs
        dots = weights * grad_probs
        near = jnp.where(is_near, 1.0, 0.0)
        near_total += weights * near
        far_total += weights * (1.0 - near)
        near_dot += dots * near
        far_dot += dots * (1.0 - near)

    def down(values):
        return jnp.sum(values, axis=1, keepdims=True)

    near_scale, far_scale = 1.0 / down(near_total), 1.0 / down(far_total)
    near_row, far_row = down(near_dot) * near_scale, down(far_dot) * far_scale
    for j in range(tiles):
        cut = slice(j * rows, (j + 1) * rows)
        is_near = j <= pair
        probs = weight_ref[:, cut] * jnp.where(is_near, near_scale, far_scale)
        squashed = squashed_ref[:, cut]
        grad_capped = probs * (grad_ref[:, cut] - jnp.where(is_near, near_row, far_row))
        both_ref[:heads, cut] = (grad_capped * (1.0 - squashed * squashed)).astype(jnp.bfloat16)
        both_ref[heads:, cut] = probs.astype(jnp.bfloat16)
        result = jnp.dot(after_ref[...], both_ref[:, cut], preferred_element_type=jnp.float32)
        kind = lax.broadcasted_iota(jnp.int32, result.shape, 0) % KINDS
        out_ref[:, cut] = jnp.where(kind < KINDS // 2, result * scaling, result).astype(jnp.bfloat16)


def grad_kernel(
    order_ref, incoming_ref, key_value_ref, spread_ref, out_ref, dense_ref, sum_ref, *, blocks, rows, strip
):
    half = blocks // 2
    group = KINDS * strip
    for p in range(blocks):
        c = pair_of(p, half, blocks)
        lane = place_of(p, 0, half, blocks, rows)
        count = (p + 1) * rows
        padded = (p // CHUNK + 1) * CHUNK * rows
        dense_ref[p * group : (p + 1) * group, :count] = incoming_ref[
            c * group : (c + 1) * group, lane : lane + count
        ]
        if padded > count:
            dense_ref[p * group : (p + 1) * group, count:padded] = jnp.zeros(
                (group, padded - count), jnp.bfloat16
            )
    for j in range(blocks // CHUNK):
        first = j * CHUNK
        cut = slice(first * rows, (first + CHUNK) * rows)
        dense = dense_ref[first * group :, cut]
        terms = lax.dot_general(
            dense,
            spread_ref[first * group :, :],
            (((0,), (0,)), ((), ())),
            preferred_element_type=jnp.float32,
        ).astype(jnp.bfloat16)
        for b in range(CHUNK):
            out_ref[order_ref[first + b], :rows, :] = terms[b * rows : (b + 1) * rows, :]
        added = jnp.dot(dense, key_value_ref[cut, :], preferred_element_type=jnp.float32)
        for kind in range(KINDS):
            columns = slice(kind * DH, (kind + 1) * DH)
            if j == 0:
                sum_ref[kind] = added[:, columns]
            else:
                sum_ref[kind, first * group : blocks * group, :] += added[:, columns]
    for kind in range(KINDS):
        columns = slice(kind * DH, (kind + 1) * DH)
        lines = sum_ref.at[kind][pl.ds(kind, blocks * strip, stride=KINDS), :].astype(jnp.bfloat16)
        for p in range(blocks):
            out_ref[order_ref[p], rows:, columns] = lines[p * strip : (p + 1) * strip, :]


def body(query_rows, key_rows, value_rows, out_grad, mix_pre, mix_post, block_order):
    blocks = lax.axis_size("seq")
    owners = lax.axis_size("row") * lax.axis_size("col")
    rows, width = query_rows.shape
    heads_local = width // DH
    heads = mix_pre.shape[0]
    scaling = DH ** (-0.5)
    strip = rows // blocks
    half = blocks // 2
    span = (blocks + 1) * rows
    seq_len = blocks * rows
    packed_rows = owners * KINDS
    spread_rows = rows * KINDS
    bf16, f32 = jnp.bfloat16, jnp.float32
    whole = pl.BlockSpec(memory_space=pltpu.VMEM)
    table = pl.BlockSpec(memory_space=pltpu.SMEM)
    exchange_shape = (blocks, rows + strip, 2 * width)

    def call(kernel, ins, outs, scratch=(), **static):
        return pl.pallas_call(
            functools.partial(kernel, **static),
            in_specs=ins,
            out_specs=[whole] * len(outs),
            out_shape=[jax.ShapeDtypeStruct(shape, bf16) for shape in outs],
            scratch_shapes=scratch,
            interpret=INTERP,
        )

    (sent,) = call(
        send_kernel, [whole] * 4, [exchange_shape], blocks=blocks, rows=rows, strip=strip, width=width
    )(query_rows, key_rows, value_rows, out_grad)
    received = lax.all_to_all(sent, "seq", split_axis=0, concat_axis=0, tiled=True)
    numbers = jnp.arange(blocks, dtype=jnp.int32)
    stored_at = jnp.sum(
        jnp.where(block_order[None, :] == numbers[:, None], numbers[None, :], 0), axis=1
    )

    packed, key_value, spread = call(
        score_kernel,
        [table, whole],
        [(packed_rows, span), (seq_len, 2 * width), (spread_rows, 2 * width)],
        [pltpu.VMEM((rows, 2 * width), f32)],
        blocks=blocks, rows=rows, strip=strip, scaling=scaling,
    )(stored_at, received)

    def exchange(values):
        return lax.all_to_all(
            values.reshape(owners, KINDS, span), HEAD_AXES, split_axis=0, concat_axis=0, tiled=True
        ).reshape(packed_rows, span)

    empty = jnp.zeros((heads, owners, heads_local), bf16)
    into_scores = jnp.concatenate([mix_pre.reshape(heads, owners, heads_local), empty], axis=2)
    into_grads = jnp.concatenate([empty, mix_post.T.reshape(heads, owners, heads_local)], axis=2)
    before = jnp.concatenate([into_scores, into_grads], axis=0).reshape(2 * heads, packed_rows)
    out_scores = mix_pre.T.reshape(owners, heads_local, heads)
    out_probs = mix_post.reshape(owners, heads_local, heads)
    blank = jnp.zeros((owners, heads_local, heads), bf16)
    after = jnp.concatenate(
        [
            jnp.concatenate([out_scores, blank], axis=1),
            jnp.concatenate([blank, out_probs], axis=1),
        ],
        axis=2,
    ).reshape(packed_rows, 2 * heads)
    own = lax.axis_index(HEAD_AXES)
    where = jnp.stack([own // strip, lax.axis_index("seq") * strip + own % strip]).astype(jnp.int32)
    (mixed,) = call(
        mix_kernel,
        [table, whole, whole, whole],
        [(packed_rows, span)],
        [
            pltpu.VMEM((heads, span), f32),
            pltpu.VMEM((heads, span), f32),
            pltpu.VMEM((heads, span), f32),
            pltpu.VMEM((2 * heads, span), bf16),
        ],
        blocks=blocks, rows=rows, heads=heads, scaling=scaling,
    )(where, exchange(packed), before, after)

    (sent,) = call(
        grad_kernel,
        [table, whole, whole, whole],
        [exchange_shape],
        [pltpu.VMEM((spread_rows, seq_len), bf16), pltpu.VMEM((KINDS, spread_rows, DH), f32)],
        blocks=blocks, rows=rows, strip=strip,
    )(stored_at, exchange(mixed), key_value, spread)
    received = lax.all_to_all(sent, "seq", split_axis=0, concat_axis=0, tiled=True)
    summed = jnp.sum(received[:, :rows].astype(f32), axis=0).astype(bf16)
    lines = received[:, rows:].reshape(rows, 2 * width)
    return (lines[:, width:], lines[:, :width], summed[:, :width], summed[:, width:])


def solution(mesh):
    spread = P("seq", HEAD_AXES)
    return jax.shard_map(
        body,
        mesh=mesh,
        in_specs=(spread, spread, spread, spread, P(), P(), P()),
        out_specs=(spread, spread, spread, spread),
        check_vma=False,
    )
```

```python
import functools

import jax
import jax.numpy as jnp
from jax import lax
from jax.experimental import pallas as pl
from jax.experimental.pallas import tpu as pltpu
from jax.sharding import PartitionSpec as P

DH = 128


logit_cap = 10.0

HEAD_AXES = ("row", "col")
KINDS = 4
CHUNK = 4
VMEM_LIMIT = 24 << 20
INTERP = False


def place_of(p, b, half, blocks, rows):
    return (b if p < half else blocks - p + b) * rows


def pair_of(p, half, blocks):
    return p if p < half else blocks - 1 - p


def send_kernel(query_ref, key_ref, value_ref, grad_ref, out_ref, *, blocks, rows, strip, width):
    for s in range(blocks):
        out_ref[s, :rows, :width] = key_ref[...]
        out_ref[s, :rows, width:] = value_ref[...]
        out_ref[s, rows:, :width] = query_ref[s * strip : (s + 1) * strip, :]
        out_ref[s, rows:, width:] = grad_ref[s * strip : (s + 1) * strip, :]


def sort_blocks(
    block_ref, received_ref, order_ref, key_value_ref, spread_ref, lines_ref, blocks, rows, strip
):
    group = KINDS * strip
    for s in range(blocks):
        order_ref[block_ref[s]] = s
    for p in range(blocks):
        source = order_ref[p]
        key_value_ref[p * rows : (p + 1) * rows, :] = received_ref[source, :rows, :]
        lines_ref[p * strip : (p + 1) * strip, :] = received_ref[source, rows:, :].astype(jnp.float32)
    total = blocks * group
    row = lax.broadcasted_iota(jnp.int32, (total, blocks * strip), 0)
    line = lax.broadcasted_iota(jnp.int32, (total, blocks * strip), 1)
    repeat = jnp.where(row // KINDS == line, 1.0, 0.0).astype(jnp.bfloat16)
    repeated = jnp.dot(
        repeat, lines_ref[...].astype(jnp.bfloat16), preferred_element_type=jnp.float32
    )
    row = lax.broadcasted_iota(jnp.int32, (total, KINDS * DH), 0)
    column = lax.broadcasted_iota(jnp.int32, (total, KINDS * DH), 1)
    spread_ref[...] = jnp.where(row % KINDS == column // DH, repeated, 0.0).astype(jnp.bfloat16)


def score_kernel(
    block_ref, received_ref, out_ref, order_ref, key_value_ref, spread_ref, lines_ref,
    *, blocks, rows, strip, scaling
):
    half = blocks // 2
    group = KINDS * strip
    sort_blocks(
        block_ref, received_ref, order_ref, key_value_ref, spread_ref, lines_ref, blocks, rows, strip
    )
    for j in range(blocks // CHUNK):
        first = j * CHUNK
        keys = key_value_ref[first * rows : (first + CHUNK) * rows, :]
        scores = lax.dot_general(
            spread_ref[first * group :, :],
            keys,
            (((1,), (1,)), ((), ())),
            preferred_element_type=jnp.float32,
        )
        kind = lax.broadcasted_iota(jnp.int32, scores.shape, 0) % KINDS
        scores = jnp.where(kind < KINDS // 2, scores * scaling, scores).astype(jnp.bfloat16)
        for p in range(first, blocks):
            count = min(p - first + 1, CHUNK)
            c = pair_of(p, half, blocks)
            lane = place_of(p, first, half, blocks, rows)
            out_ref[c * strip : (c + 1) * strip, :, lane : lane + count * rows] = scores[
                (p - first) * group : (p - first + 1) * group, : count * rows
            ].reshape(strip, KINDS, count * rows)


def mix_kernel(
    incoming_ref, pre_ref, post_ref, out_ref, before_ref, after_ref, squashed_ref, weight_ref, grad_ref,
    both_ref, *, blocks, rows, strip, heads, scaling
):
    own = lax.axis_index(HEAD_AXES)
    pair = lax.div(own, strip)
    offset = lax.axis_index("seq") * strip + lax.rem(own, strip)
    shape = (heads, before_ref.shape[1])
    row = lax.broadcasted_iota(jnp.int32, shape, 0)
    column = lax.broadcasted_iota(jnp.int32, shape, 1)
    kind = column % KINDS
    here = column // KINDS * (KINDS // 2) + kind % (KINDS // 2) == row
    pick_scores = jnp.where(here & (kind < KINDS // 2), 1.0, 0.0).astype(jnp.bfloat16)
    pick_probs = jnp.where(here & (kind >= KINDS // 2), 1.0, 0.0).astype(jnp.bfloat16)

    def pick(left, right, left_dim, right_dim):
        return lax.dot_general(
            left,
            right,
            (((left_dim,), (right_dim,)), ((), ())),
            preferred_element_type=jnp.float32,
        ).astype(jnp.bfloat16)

    pre, post = pre_ref[...], post_ref[...]
    before_ref[:heads, :] = pick(pre, pick_scores, 1, 0)
    before_ref[heads:, :] = pick(post, pick_probs, 0, 0)
    after_ref[:, :heads] = pick(pick_scores, pre, 0, 1)
    after_ref[:, heads:] = pick(pick_probs, post, 0, 0)
    zero = jnp.zeros((heads, rows), jnp.float32)
    near_total, far_total, near_dot, far_dot = zero, zero, zero, zero
    lane = lax.broadcasted_iota(jnp.int32, (heads, rows), 1)
    tiles = blocks + 1
    for j in range(tiles):
        cut = slice(j * rows, (j + 1) * rows)
        mixed = jnp.dot(
            before_ref[...], incoming_ref[:, :, cut].reshape(before_ref.shape[1], rows), preferred_element_type=jnp.float32
        )
        is_near = j <= pair
        start = (j - jnp.where(is_near, 0, pair + 1)) * rows
        limit = jnp.where(is_near, pair, blocks - 1 - pair) * rows + offset - start
        squashed = jnp.tanh(mixed[:heads] / logit_cap)
        weights = jnp.where(lane <= limit, jnp.exp(logit_cap * squashed), 0.0)
        grad_probs = mixed[heads:]
        squashed_ref[:, cut] = squashed
        weight_ref[:, cut] = weights
        grad_ref[:, cut] = grad_probs
        dots = weights * grad_probs
        near = jnp.where(is_near, 1.0, 0.0)
        near_total += weights * near
        far_total += weights * (1.0 - near)
        near_dot += dots * near
        far_dot += dots * (1.0 - near)

    def down(values):
        return jnp.sum(values, axis=1, keepdims=True)

    near_scale, far_scale = 1.0 / down(near_total), 1.0 / down(far_total)
    near_row, far_row = down(near_dot) * near_scale, down(far_dot) * far_scale
    for j in range(tiles):
        cut = slice(j * rows, (j + 1) * rows)
        is_near = j <= pair
        probs = weight_ref[:, cut] * jnp.where(is_near, near_scale, far_scale)
        squashed = squashed_ref[:, cut]
        grad_capped = probs * (grad_ref[:, cut] - jnp.where(is_near, near_row, far_row))
        both_ref[:heads, cut] = (grad_capped * (1.0 - squashed * squashed)).astype(jnp.bfloat16)
        both_ref[heads:, cut] = probs.astype(jnp.bfloat16)
        result = jnp.dot(after_ref[...], both_ref[:, cut], preferred_element_type=jnp.float32)
        kind = lax.broadcasted_iota(jnp.int32, result.shape, 0) % KINDS
        out_ref[:, :, cut] = jnp.where(kind < KINDS // 2, result * scaling, result).astype(jnp.bfloat16).reshape(out_ref.shape[0], KINDS, rows)


def grad_kernel(
    block_ref, incoming_ref, received_ref, out_ref, dense_ref, sum_ref, order_ref, key_value_ref,
    spread_ref, lines_ref,
    *, blocks, rows, strip
):
    half = blocks // 2
    group = KINDS * strip
    sort_blocks(
        block_ref, received_ref, order_ref, key_value_ref, spread_ref, lines_ref, blocks, rows, strip
    )
    for p in range(blocks):
        c = pair_of(p, half, blocks)
        lane = place_of(p, 0, half, blocks, rows)
        count = (p + 1) * rows
        padded = (p // CHUNK + 1) * CHUNK * rows
        dense_ref[p * group : (p + 1) * group, :count] = incoming_ref[
            c * strip : (c + 1) * strip, :, lane : lane + count
        ].reshape(group, count)
        if padded > count:
            dense_ref[p * group : (p + 1) * group, count:padded] = jnp.zeros(
                (group, padded - count), jnp.bfloat16
            )
    for j in range(blocks // CHUNK):
        first = j * CHUNK
        cut = slice(first * rows, (first + CHUNK) * rows)
        dense = dense_ref[first * group :, cut]
        terms = lax.dot_general(
            dense,
            spread_ref[first * group :, :],
            (((0,), (0,)), ((), ())),
            preferred_element_type=jnp.float32,
        ).astype(jnp.bfloat16)
        for b in range(CHUNK):
            out_ref[order_ref[first + b], :rows, :] = terms[b * rows : (b + 1) * rows, :]
        added = jnp.dot(dense, key_value_ref[cut, :], preferred_element_type=jnp.float32)
        for kind in range(KINDS):
            columns = slice(kind * DH, (kind + 1) * DH)
            if j == 0:
                sum_ref[kind] = added[:, columns]
            else:
                sum_ref[kind, first * group : blocks * group, :] += added[:, columns]
    for kind in range(KINDS):
        columns = slice(kind * DH, (kind + 1) * DH)
        lines = sum_ref.at[kind][pl.ds(kind, blocks * strip, stride=KINDS), :].astype(jnp.bfloat16)
        for p in range(blocks):
            out_ref[order_ref[p], rows:, columns] = lines[p * strip : (p + 1) * strip, :]


def body(query_rows, key_rows, value_rows, out_grad, mix_pre, mix_post, block_order):
    blocks = lax.axis_size("seq")
    owners = lax.axis_size("row") * lax.axis_size("col")
    rows, width = query_rows.shape
    heads_local = width // DH
    heads = mix_pre.shape[0]
    scaling = DH ** (-0.5)
    strip = rows // blocks
    half = blocks // 2
    span = (blocks + 1) * rows
    seq_len = blocks * rows
    packed_rows = owners * KINDS
    spread_rows = rows * KINDS
    bf16, f32 = jnp.bfloat16, jnp.float32
    whole = pl.BlockSpec(memory_space=pltpu.VMEM)
    table = pl.BlockSpec(memory_space=pltpu.SMEM)
    exchange_shape = (blocks, rows + strip, 2 * width)

    def call(kernel, ins, outs, scratch=(), **static):
        return pl.pallas_call(
            functools.partial(kernel, **static),
            in_specs=ins,
            out_specs=[whole] * len(outs),
            out_shape=[jax.ShapeDtypeStruct(shape, bf16) for shape in outs],
            scratch_shapes=scratch,
            compiler_params=pltpu.CompilerParams(vmem_limit_bytes=VMEM_LIMIT),
            interpret=INTERP,
        )

    def near(values):
        if INTERP:
            return values
        return pltpu.with_memory_space_constraint(values, pltpu.VMEM)

    (sent,) = call(
        send_kernel, [whole] * 4, [exchange_shape], blocks=blocks, rows=rows, strip=strip, width=width
    )(query_rows, key_rows, value_rows, out_grad)
    received = near(lax.all_to_all(sent, "seq", split_axis=0, concat_axis=0, tiled=True))

    sorted_blocks = [
        pltpu.SMEM((blocks,), jnp.int32),
        pltpu.VMEM((seq_len, 2 * width), bf16),
        pltpu.VMEM((spread_rows, 2 * width), bf16),
        pltpu.VMEM((rows, 2 * width), f32),
    ]
    (packed,) = call(
        score_kernel,
        [table, whole],
        [(owners, KINDS, span)],
        sorted_blocks,
        blocks=blocks, rows=rows, strip=strip, scaling=scaling,
    )(block_order, received)

    def exchange(values):
        return near(lax.all_to_all(values, HEAD_AXES, split_axis=0, concat_axis=0, tiled=True))

    (mixed,) = call(
        mix_kernel,
        [whole, whole, whole],
        [(owners, KINDS, span)],
        [
            pltpu.VMEM((2 * heads, packed_rows), bf16),
            pltpu.VMEM((packed_rows, 2 * heads), bf16),
            pltpu.VMEM((heads, span), f32),
            pltpu.VMEM((heads, span), f32),
            pltpu.VMEM((heads, span), f32),
            pltpu.VMEM((2 * heads, span), bf16),
        ],
        blocks=blocks, rows=rows, strip=strip, heads=heads, scaling=scaling,
    )(exchange(packed), mix_pre, mix_post)

    (sent,) = call(
        grad_kernel,
        [table, whole, whole],
        [exchange_shape],
        [pltpu.VMEM((spread_rows, seq_len), bf16), pltpu.VMEM((KINDS, spread_rows, DH), f32)]
        + sorted_blocks,
        blocks=blocks, rows=rows, strip=strip,
    )(block_order, exchange(mixed), received)
    received = lax.all_to_all(sent, "seq", split_axis=0, concat_axis=0, tiled=True)
    summed = jnp.sum(received[:, :rows].astype(f32), axis=0).astype(bf16)
    lines = received[:, rows:].reshape(rows, 2 * width)
    return (lines[:, width:], lines[:, :width], summed[:, :width], summed[:, width:])


def solution(mesh):
    spread = P("seq", HEAD_AXES)
    return jax.shard_map(
        body,
        mesh=mesh,
        in_specs=(spread, spread, spread, spread, P(), P(), P()),
        out_specs=(spread, spread, spread, spread),
        check_vma=False,
    )
```

```python
import functools

import jax
import jax.numpy as jnp
from jax import lax
from jax.experimental import pallas as pl
from jax.experimental.pallas import tpu as pltpu
from jax.sharding import PartitionSpec as P

DH = 128


logit_cap = 10.0

HEAD_AXES = ("row", "col")
HEADS = 2
CHUNK = 4
VMEM_LIMIT = 24 << 20
INTERP = False
BF16, F32 = jnp.bfloat16, jnp.float32


def dot(left, right, left_dim=1, right_dim=0):
    return lax.dot_general(
        left, right, (((left_dim,), (right_dim,)), ((), ())), preferred_element_type=F32
    )


def iota(shape, dim):
    return lax.broadcasted_iota(jnp.int32, shape, dim)


def to_strips(blocks, strip):
    shape = (blocks * strip, blocks * strip)
    row, column = iota(shape, 0), iota(shape, 1)
    return jnp.where(row % strip * blocks + row // strip == column, 1.0, 0.0).astype(BF16)


def to_slots(blocks, strip):
    shape = (blocks * strip * HEADS, blocks * strip)
    row, column = iota(shape, 0), iota(shape, 1)
    block, slot = row // (strip * HEADS), row // HEADS % strip
    line = jnp.where(block < blocks // 2, slot, strip - 1 - slot)
    return jnp.where(block * strip + line == column, 1.0, 0.0).astype(BF16)


def own_head(shape):
    return iota(shape, 0) % HEADS == iota(shape, 1) // DH % HEADS


def send_kernel(
    query_hbm, key_hbm, value_hbm, grad_hbm, out_ref, query_ref, key_ref, value_ref, grad_ref, sems,
    *, blocks, rows, strip, width
):
    copies = [
        pltpu.make_async_copy(source, target, sems.at[n])
        for n, (source, target) in enumerate(
            [
                (query_hbm, query_ref),
                (grad_hbm, grad_ref),
                (key_hbm, key_ref),
                (value_hbm, value_ref),
            ]
        )
    ]
    for copy in copies:
        copy.start()
    pick = to_strips(blocks, strip)
    for copy in copies:
        copy.wait()
    queries = dot(pick, query_ref[...])
    grads = dot(pick, grad_ref[...])
    for s in range(blocks):
        out_ref[s, :rows, :width] = key_ref[...]
        out_ref[s, :rows, width:] = value_ref[...]
        out_ref[s, rows:, :width] = queries[s * strip : (s + 1) * strip, :].astype(BF16)
        out_ref[s, rows:, width:] = grads[s * strip : (s + 1) * strip, :].astype(BF16)


def sort_blocks(
    block_ref, received_ref, order_ref, key_value_ref, spread_ref, lines_ref, blocks, rows, strip
):
    for s in range(blocks):
        order_ref[block_ref[s]] = s
    for p in range(blocks):
        source = order_ref[p]
        key_value_ref[p * rows : (p + 1) * rows, :] = received_ref[source, :rows, :]
        lines_ref[p * strip : (p + 1) * strip, :] = received_ref[source, rows:, :].astype(F32)
    spread = dot(to_slots(blocks, strip), lines_ref[...].astype(BF16))
    spread_ref[...] = jnp.where(own_head(spread.shape), spread, 0.0).astype(BF16)


def score_kernel(
    block_ref, received_ref, out_ref, order_ref, key_value_ref, spread_ref, lines_ref, diagonal_ref,
    *, blocks, rows, strip, width, scaling
):
    half = blocks // 2
    group = HEADS * strip
    sort_blocks(
        block_ref, received_ref, order_ref, key_value_ref, spread_ref, lines_ref, blocks, rows, strip
    )
    for kind in range(2):
        columns = slice(kind * width, (kind + 1) * width)
        base = kind * blocks * rows
        for j in range(blocks // CHUNK):
            first = j * CHUNK
            scores = dot(
                spread_ref[first * group :, columns],
                key_value_ref[first * rows : (first + CHUNK) * rows, columns],
                1,
                1,
            )
            if kind == 0:
                scores = scores * scaling
            for p in range(first, blocks):
                piece = scores[(p - first) * group : (p - first + 1) * group, :]
                count = min(p - first, CHUNK)
                if p - first < CHUNK:
                    diagonal_ref[kind, p] = piece[:, count * rows : (count + 1) * rows]
                if count:
                    c = min(p, blocks - 1 - p)
                    lane = base + (first if p < half else blocks - 1 - p + first) * rows
                    out_ref[c * strip : (c + 1) * strip, :, lane : lane + count * rows] = (
                        piece[:, : count * rows].astype(BF16).reshape(strip, HEADS, count * rows)
                    )
    low = iota((group, rows), 1) < rows // 2
    for c in range(half):
        cut = slice(c * strip, (c + 1) * strip)
        halves = []
        for kind in range(2):
            near, far = diagonal_ref[kind, c], diagonal_ref[kind, blocks - 1 - c]
            full = jnp.concatenate([far[:strip], near[strip:]], axis=0)
            halves.append(jnp.concatenate([near[:strip], far[strip:]], axis=0))
            lane = ((kind + 1) * blocks - 1) * rows
            out_ref[cut, :, lane : lane + rows] = full.astype(BF16).reshape(strip, HEADS, rows)
        joined = jnp.where(low, halves[0], roll(halves[1], rows // 2))
        lane = 2 * blocks * rows
        out_ref[cut, :, lane:] = joined.astype(BF16).reshape(strip, HEADS, rows)


def roll(values, shift):
    if INTERP:
        return jnp.roll(values, shift, 1)
    return pltpu.roll(values, shift, 1)


def mix_kernel(
    incoming_ref, pre_ref, post_ref, out_ref, mixed_ref, grad_ref, both_ref,
    *, blocks, rows, strip, heads, scaling
):
    own = lax.axis_index(HEAD_AXES)
    pair, line = lax.div(own, strip), lax.rem(own, strip)
    seq = lax.axis_index("seq")
    near_offset = line * blocks + seq
    far_offset = (strip - 1 - line) * blocks + seq
    owners = heads // HEADS
    seq_len = blocks * rows
    pre, post = pre_ref[...], post_ref[...]
    extra = incoming_ref[:, :, 2 * seq_len :].reshape(heads, rows)
    mixed_ref[:, :seq_len] = dot(pre, incoming_ref[:, :, :seq_len].reshape(heads, seq_len))
    mixed_ref[:, seq_len:] = dot(pre, extra)
    grad_ref[:, :seq_len] = dot(
        post, incoming_ref[:, :, seq_len : 2 * seq_len].reshape(heads, seq_len), 0, 0
    )
    grad_ref[:, seq_len:] = roll(dot(post, extra, 0, 0), rows // 2)

    lane = iota((heads, rows), 1)
    early = line < strip // 2
    is_near = [j < pair for j in range(blocks - 1)]
    is_near += [jnp.logical_not(early), early]
    limits = [None] * (blocks - 1)
    limits += [jnp.where(near, near_offset, far_offset) for near in is_near[blocks - 1 :]]
    zero = jnp.zeros((heads, rows), F32)
    near_total, far_total, near_dot, far_dot = zero, zero, zero, zero
    squashed_tiles = []
    for j in range(blocks + 1):
        cut = slice(j * rows, (j + 1) * rows)
        squashed = jnp.tanh(mixed_ref[:, cut] / logit_cap)
        weights = jnp.exp(logit_cap * squashed)
        grads = grad_ref[:, cut]
        if limits[j] is not None:
            weights = jnp.where(lane <= limits[j], weights, 0.0)
        dots = weights * grads
        mixed_ref[:, cut] = weights
        grad_ref[:, cut] = grads
        squashed_tiles.append(squashed)
        near = jnp.where(is_near[j], 1.0, 0.0)
        near_total += weights * near
        far_total += weights * (1.0 - near)
        near_dot += dots * near
        far_dot += dots * (1.0 - near)

    def down(values):
        return jnp.sum(values, axis=1, keepdims=True)

    near_scale, far_scale = 1.0 / down(near_total), 1.0 / down(far_total)
    near_row, far_row = down(near_dot) * near_scale, down(far_dot) * far_scale
    for j in range(blocks + 1):
        cut = slice(j * rows, (j + 1) * rows)
        probs = mixed_ref[:, cut] * jnp.where(is_near[j], near_scale, far_scale)
        squashed = squashed_tiles[j]
        grad_capped = probs * (grad_ref[:, cut] - jnp.where(is_near[j], near_row, far_row))
        both_ref[0, :, cut] = (grad_capped * (1.0 - squashed * squashed)).astype(BF16)
        both_ref[1, :, cut] = probs.astype(BF16)
    grad_scores = dot(pre, both_ref[0], 0, 0) * scaling
    post_mixed = dot(post, both_ref[1])
    joined = jnp.where(
        lane < rows // 2, grad_scores[:, seq_len:], roll(post_mixed[:, seq_len:], rows // 2)
    )
    shape = (owners, HEADS, seq_len)
    out_ref[:, :, :seq_len] = grad_scores[:, :seq_len].astype(BF16).reshape(shape)
    out_ref[:, :, seq_len : 2 * seq_len] = post_mixed[:, :seq_len].astype(BF16).reshape(shape)
    out_ref[:, :, 2 * seq_len :] = joined.astype(BF16).reshape(owners, HEADS, rows)


def grad_kernel(
    block_ref, incoming_ref, received_ref, out_ref, dense_ref, sum_ref, order_ref, key_value_ref,
    spread_ref, lines_ref, *, blocks, rows, strip, width
):
    half = blocks // 2
    group = HEADS * strip
    sort_blocks(
        block_ref, received_ref, order_ref, key_value_ref, spread_ref, lines_ref, blocks, rows, strip
    )
    low = iota((group, rows), 1) < rows // 2
    for c in range(half):
        own = slice(c * strip, (c + 1) * strip)
        extra = incoming_ref[own, :, 2 * blocks * rows :].reshape(group, rows).astype(F32)
        for kind in range(2):
            base = kind * blocks * rows
            last = base + (blocks - 1) * rows
            full = incoming_ref[own, :, last : last + rows].reshape(group, rows).astype(F32)
            part = extra if kind == 0 else roll(extra, rows // 2)
            part = jnp.where(low, part, 0.0)
            near = jnp.concatenate([part[:strip], full[strip:]], axis=0)
            far = jnp.concatenate([full[:strip], part[strip:]], axis=0)
            for p, diagonal, lane in ((c, near, base), (blocks - 1 - c, far, base + c * rows)):
                slots = slice(p * group, (p + 1) * group)
                if p:
                    dense_ref[kind, slots, : p * rows] = incoming_ref[
                        own, :, lane : lane + p * rows
                    ].reshape(group, p * rows)
                dense_ref[kind, slots, p * rows : (p + 1) * rows] = diagonal.astype(BF16)
                reach = (p // CHUNK + 1) * CHUNK * rows
                if reach > (p + 1) * rows:
                    dense_ref[kind, slots, (p + 1) * rows : reach] = jnp.zeros(
                        (group, reach - (p + 1) * rows), BF16
                    )
    gather = to_slots(blocks, strip)
    for kind in range(2):
        columns = slice(kind * width, (kind + 1) * width)
        for j in range(blocks // CHUNK):
            first = j * CHUNK
            cut = slice(first * rows, (first + CHUNK) * rows)
            dense = dense_ref[kind, first * group :, cut]
            terms = dot(dense, spread_ref[first * group :, columns], 0, 0).astype(BF16)
            for b in range(CHUNK):
                out_ref[order_ref[first + b], :rows, columns] = terms[b * rows : (b + 1) * rows, :]
            added = dot(dense, key_value_ref[cut, columns])
            if j == 0:
                sum_ref[...] = added
            else:
                sum_ref[first * group :, :] = sum_ref[first * group :, :] + added
        found = jnp.where(own_head(sum_ref.shape), sum_ref[...], 0.0).astype(BF16)
        lines = dot(gather, found, 0, 0).astype(BF16)
        for p in range(blocks):
            out_ref[order_ref[p], rows:, columns] = lines[p * strip : (p + 1) * strip, :]


def final_kernel(
    received_ref, attended_ref, query_ref, key_ref, value_ref, lines_ref, *, blocks, rows, strip, width
):
    total = received_ref[0, :rows, :].astype(F32)
    for s in range(1, blocks):
        total += received_ref[s, :rows, :].astype(F32)
    for s in range(blocks):
        lines_ref[s * strip : (s + 1) * strip, :] = received_ref[s, rows:, :].astype(F32)
    lines = dot(to_strips(blocks, strip), lines_ref[...].astype(BF16), 0, 0).astype(BF16)
    query_ref[...] = lines[:, :width]
    attended_ref[...] = lines[:, width:]
    key_ref[...] = total[:, :width].astype(BF16)
    value_ref[...] = total[:, width:].astype(BF16)


def body(query_rows, key_rows, value_rows, out_grad, mix_pre, mix_post, block_order):
    blocks = lax.axis_size("seq")
    owners = lax.axis_size("row") * lax.axis_size("col")
    rows, width = query_rows.shape
    heads = mix_pre.shape[0]
    scaling = DH ** (-0.5)
    strip = rows // blocks
    span = (blocks + 1) * rows
    seq_len = blocks * rows
    slots = rows * HEADS
    whole = pl.BlockSpec(memory_space=pltpu.VMEM)
    table = pl.BlockSpec(memory_space=pltpu.SMEM)
    seq_shape = (blocks, rows + strip, 2 * width)
    head_shape = (owners, HEADS, (2 * blocks + 1) * rows)
    static = dict(blocks=blocks, rows=rows, strip=strip)

    def call(kernel, ins, outs, scratch=(), **more):
        return pl.pallas_call(
            functools.partial(kernel, **static, **more),
            in_specs=ins,
            out_specs=[whole] * len(outs),
            out_shape=[jax.ShapeDtypeStruct(shape, BF16) for shape in outs],
            scratch_shapes=scratch,
            compiler_params=pltpu.CompilerParams(vmem_limit_bytes=VMEM_LIMIT),
            interpret=INTERP,
        )

    def exchange(values, axes):
        values = lax.all_to_all(values, axes, split_axis=0, concat_axis=0, tiled=True)
        if INTERP:
            return values
        return pltpu.with_memory_space_constraint(values, pltpu.VMEM)

    def far(values):
        return values if INTERP else pltpu.with_memory_space_constraint(values, pltpu.HBM)

    (sent,) = call(
        send_kernel,
        [pl.BlockSpec(memory_space=pltpu.HBM)] * 4,
        [seq_shape],
        [pltpu.VMEM((rows, width), BF16)] * 4 + [pltpu.SemaphoreType.DMA((4,))],
        width=width,
    )(*[far(values) for values in (query_rows, key_rows, value_rows, out_grad)])
    received = exchange(sent, "seq")
    sorted_blocks = [
        pltpu.SMEM((blocks,), jnp.int32),
        pltpu.VMEM((seq_len, 2 * width), BF16),
        pltpu.VMEM((slots, 2 * width), BF16),
        pltpu.VMEM((rows, 2 * width), F32),
    ]
    (packed,) = call(
        score_kernel,
        [table, whole],
        [head_shape],
        sorted_blocks + [pltpu.VMEM((2, blocks, HEADS * strip, rows), F32)],
        width=width, scaling=scaling,
    )(block_order, received)
    (mixed,) = call(
        mix_kernel,
        [whole] * 3,
        [head_shape],
        [
            pltpu.VMEM((heads, span), F32),
            pltpu.VMEM((heads, span), F32),
            pltpu.VMEM((2, heads, span), BF16),
        ],
        heads=heads, scaling=scaling,
    )(exchange(packed, HEAD_AXES), mix_pre, mix_post)
    (sent,) = call(
        grad_kernel,
        [table, whole, whole],
        [seq_shape],
        [pltpu.VMEM((2, slots, seq_len), BF16), pltpu.VMEM((slots, width), F32)] + sorted_blocks,
        width=width,
    )(block_order, exchange(mixed, HEAD_AXES), received)
    return call(
        final_kernel,
        [whole],
        [(rows, width)] * 4,
        [pltpu.VMEM((rows, 2 * width), F32)],
        width=width,
    )(exchange(sent, "seq"))


def solution(mesh):
    spread = P("seq", HEAD_AXES)
    return jax.shard_map(
        body,
        mesh=mesh,
        in_specs=(spread, spread, spread, spread, P(), P(), P()),
        out_specs=(spread, spread, spread, spread),
        check_vma=False,
    )
```

```python
import functools

import jax
import jax.numpy as jnp
from jax import lax
from jax.experimental import pallas as pl
from jax.experimental.pallas import tpu as pltpu
from jax.sharding import PartitionSpec as P

DH = 128


logit_cap = 10.0

HEAD_AXES = ("row", "col")
HEADS = 2
CHUNK = 2
SPLIT = 2
VMEM_LIMIT = 24 << 20
INTERP = False
BF16, F32 = jnp.bfloat16, jnp.float32


def dot(left, right, left_dim=1, right_dim=0):
    return lax.dot_general(
        left, right, (((left_dim,), (right_dim,)), ((), ())), preferred_element_type=F32
    )


def iota(shape, dim):
    return lax.broadcasted_iota(jnp.int32, shape, dim)


def to_classes(rows, classes):
    row, column = iota((rows, rows), 0), iota((rows, rows), 1)
    per = rows // classes
    return jnp.where(row % per * classes + row // per == column, 1.0, 0.0).astype(BF16)


def to_slots(supers, reach):
    shape = (supers * reach * HEADS, supers * reach)
    row, column = iota(shape, 0), iota(shape, 1)
    block, slot = row // (reach * HEADS), row // HEADS % reach
    line = jnp.where(block < supers // 2, slot, reach - 1 - slot)
    return jnp.where(block * reach + line == column, 1.0, 0.0).astype(BF16)


def own_head(shape):
    return iota(shape, 0) % HEADS == iota(shape, 1) // DH % HEADS


def send_kernel(
    query_hbm, key_hbm, value_hbm, grad_hbm, out_ref, query_ref, key_ref, value_ref, grad_ref, sems,
    *, blocks, rows, strip, width
):
    copies = [
        pltpu.make_async_copy(source, target, sems.at[n])
        for n, (source, target) in enumerate(
            [
                (query_hbm, query_ref),
                (grad_hbm, grad_ref),
                (key_hbm, key_ref),
                (value_hbm, value_ref),
            ]
        )
    ]
    for copy in copies:
        copy.start()
    pick_keys, pick_lines = to_classes(rows, SPLIT), to_classes(rows, blocks // SPLIT)
    for copy in copies:
        copy.wait()
    queries = dot(pick_lines, query_ref[...]).astype(BF16)
    grads = dot(pick_lines, grad_ref[...]).astype(BF16)
    keys = dot(pick_keys, key_ref[...]).astype(BF16)
    values = dot(pick_keys, value_ref[...]).astype(BF16)
    part = rows // SPLIT
    for s in range(blocks):
        key_cut = slice(s % SPLIT * part, (s % SPLIT + 1) * part)
        line_cut = slice(s // SPLIT * strip, (s // SPLIT + 1) * strip)
        out_ref[s, :part, :width] = keys[key_cut, :]
        out_ref[s, :part, width:] = values[key_cut, :]
        out_ref[s, part:, :width] = queries[line_cut, :]
        out_ref[s, part:, width:] = grads[line_cut, :]


def sort_blocks(
    block_ref, received_ref, order_ref, key_value_ref, spread_ref, lines_ref, blocks, rows, strip
):
    part = rows // SPLIT
    for s in range(blocks):
        order_ref[block_ref[s]] = s
    for p in range(blocks):
        source = order_ref[p]
        key_value_ref[p * part : (p + 1) * part, :] = received_ref[source, :part, :]
        lines_ref[p * strip : (p + 1) * strip, :] = received_ref[source, part:, :].astype(F32)
    spread = dot(to_slots(blocks // SPLIT, strip * SPLIT), lines_ref[...].astype(BF16))
    spread_ref[...] = jnp.where(own_head(spread.shape), spread, 0.0).astype(BF16)


def score_kernel(
    block_ref, received_ref, out_ref, order_ref, key_value_ref, spread_ref, lines_ref, diagonal_ref,
    *, blocks, rows, strip, width, scaling
):
    supers = blocks // SPLIT
    half = supers // 2
    per = strip * SPLIT // 2
    side = per * HEADS
    group = 2 * side
    tiles = 2 * supers + 1
    sort_blocks(
        block_ref, received_ref, order_ref, key_value_ref, spread_ref, lines_ref, blocks, rows, strip
    )
    for kind in range(2):
        columns = slice(kind * width, (kind + 1) * width)
        for j in range(supers // CHUNK):
            first = j * CHUNK
            scores = dot(
                spread_ref[first * group :, columns],
                key_value_ref[first * rows : (first + CHUNK) * rows, columns],
                1,
                1,
            )
            if kind == 0:
                scores = scores * scaling
            for p in range(first, supers):
                piece = scores[(p - first) * group : (p - first + 1) * group, :]
                count = min(p - first, CHUNK)
                if p - first < CHUNK:
                    diagonal_ref[kind, p] = piece[:, count * rows : (count + 1) * rows]
                if count:
                    c = min(p, supers - 1 - p)
                    skip = kind * supers + (first if p < half else supers - 1 - p + first)
                    for u in range(2):
                        lane = (u * tiles + skip) * rows
                        out_ref[c * per : (c + 1) * per, :, lane : lane + count * rows] = (
                            piece[u * side : (u + 1) * side, : count * rows]
                            .astype(BF16)
                            .reshape(per, HEADS, count * rows)
                        )
    low = iota((side, rows), 1) < rows // 2
    for c in range(half):
        cut = slice(c * per, (c + 1) * per)
        for u in range(2):
            own = slice(u * side, (u + 1) * side)
            halves = []
            for kind in range(2):
                near = diagonal_ref[kind, c, own]
                far = diagonal_ref[kind, supers - 1 - c, own]
                full, part = (near, far) if u else (far, near)
                halves.append(part)
                lane = (u * tiles + (kind + 1) * supers - 1) * rows
                out_ref[cut, :, lane : lane + rows] = full.astype(BF16).reshape(per, HEADS, rows)
            joined = jnp.where(low, halves[0], roll(halves[1], rows // 2))
            lane = (u * tiles + 2 * supers) * rows
            out_ref[cut, :, lane : lane + rows] = joined.astype(BF16).reshape(per, HEADS, rows)


def roll(values, shift):
    if INTERP:
        return jnp.roll(values, shift, 1)
    return pltpu.roll(values, shift, 1)


def near_tiles(pair, supers, u):
    return [j < pair for j in range(supers - 1)] + [u == 1, u == 0]


def weigh_kernel(
    incoming_ref, pre_ref, post_ref, weight_ref, squashed_ref, grad_ref, sum_ref,
    *, blocks, rows, strip, heads
):
    supers = blocks // SPLIT
    per = strip * SPLIT // 2
    own = lax.axis_index(HEAD_AXES)
    pair, slot = lax.div(own, per), lax.rem(own, per)
    seq = lax.axis_index("seq")
    line_class, key_class = lax.div(seq, SPLIT), lax.rem(seq, SPLIT)
    pre, post = pre_ref[...], post_ref[...]
    lane = iota((heads, rows), 1)
    full = supers * rows
    sums = jnp.zeros((heads, rows), F32)
    for u in range(2):
        base = u * (2 * supers + 1) * rows
        mine = u * (supers + 1) * rows
        extra = incoming_ref[:, :, base + 2 * full : base + 2 * full + rows].reshape(heads, rows)
        squashed_ref[:, mine : mine + full] = dot(
            pre, incoming_ref[:, :, base : base + full].reshape(heads, full)
        )
        squashed_ref[:, mine + full : mine + full + rows] = dot(pre, extra)
        grad_ref[:, mine : mine + full] = dot(
            post, incoming_ref[:, :, base + full : base + 2 * full].reshape(heads, full), 0, 0
        )
        grad_ref[:, mine + full : mine + full + rows] = roll(dot(post, extra, 0, 0), rows // 2)
        line = slot + u * per
        limits = []
        for at in (line, 2 * per - 1 - line):
            offset = at * (blocks // SPLIT) + line_class
            limits.append(lax.div(offset - key_class + SPLIT, SPLIT) - 1)
        is_near = near_tiles(pair, supers, u)
        zero = jnp.zeros((heads, rows), F32)
        parts = [zero, zero, zero, zero]
        for j in range(supers + 1):
            cut = slice(mine + j * rows, mine + (j + 1) * rows)
            squashed = jnp.tanh(squashed_ref[:, cut] / logit_cap)
            weights = jnp.exp(logit_cap * squashed)
            if j >= supers - 1:
                weights = jnp.where(lane <= limits[0 if is_near[j] else 1], weights, 0.0)
            squashed_ref[:, cut] = squashed
            weight_ref[:, cut] = weights
            dots = weights * grad_ref[:, cut]
            near = jnp.where(is_near[j], 1.0, 0.0)
            for n, values in enumerate((weights, dots)):
                parts[2 * n] += values * near
                parts[2 * n + 1] += values * (1.0 - near)
        for n, values in enumerate(parts):
            down = jnp.sum(values, axis=1, keepdims=True)
            sums += jnp.where(lane == 4 * u + n, down, 0.0)
    sum_ref[...] = sums


def mix_kernel(
    weight_ref, squashed_ref, grad_ref, own_ref, other_ref, pre_ref, post_ref, out_ref, both_ref,
    *, blocks, rows, strip, heads, scaling
):
    supers = blocks // SPLIT
    per = strip * SPLIT // 2
    pair = lax.div(lax.axis_index(HEAD_AXES), per)
    owners = heads // HEADS
    full = supers * rows
    pre, post = pre_ref[...], post_ref[...]
    lane = iota((heads, rows), 1)
    sums = own_ref[...] + other_ref[...]
    for u in range(2):
        base = u * (2 * supers + 1) * rows
        mine = u * (supers + 1) * rows
        near_total, far_total, near_dot, far_dot = [
            jnp.sum(jnp.where(lane == 4 * u + n, sums, 0.0), axis=1, keepdims=True)
            for n in range(4)
        ]
        near_scale, far_scale = 1.0 / near_total, 1.0 / far_total
        near_row, far_row = near_dot * near_scale, far_dot * far_scale
        is_near = near_tiles(pair, supers, u)
        for j in range(supers + 1):
            cut = slice(mine + j * rows, mine + (j + 1) * rows)
            probs = weight_ref[:, cut] * jnp.where(is_near[j], near_scale, far_scale)
            squashed = squashed_ref[:, cut]
            grad_capped = probs * (grad_ref[:, cut] - jnp.where(is_near[j], near_row, far_row))
            both_ref[0, :, cut] = (grad_capped * (1.0 - squashed * squashed)).astype(BF16)
            both_ref[1, :, cut] = probs.astype(BF16)
        cut = slice(mine, mine + full + rows)
        grad_scores = dot(pre, both_ref[0, :, cut], 0, 0) * scaling
        post_mixed = dot(post, both_ref[1, :, cut])
        joined = jnp.where(
            lane < rows // 2, grad_scores[:, full:], roll(post_mixed[:, full:], rows // 2)
        )
        shape = (owners, HEADS, full)
        out_ref[:, :, base : base + full] = grad_scores[:, :full].astype(BF16).reshape(shape)
        out_ref[:, :, base + full : base + 2 * full] = (
            post_mixed[:, :full].astype(BF16).reshape(shape)
        )
        out_ref[:, :, base + 2 * full : base + 2 * full + rows] = joined.astype(BF16).reshape(
            owners, HEADS, rows
        )


def grad_kernel(
    block_ref, incoming_ref, received_ref, out_ref, dense_ref, sum_ref, order_ref, key_value_ref,
    spread_ref, lines_ref, *, blocks, rows, strip, width
):
    supers = blocks // SPLIT
    half = supers // 2
    per = strip * SPLIT // 2
    side = per * HEADS
    group = 2 * side
    tiles = 2 * supers + 1
    part = rows // SPLIT
    sort_blocks(
        block_ref, received_ref, order_ref, key_value_ref, spread_ref, lines_ref, blocks, rows, strip
    )
    low = iota((side, rows), 1) < rows // 2
    for c in range(half):
        own = slice(c * per, (c + 1) * per)
        for u in range(2):
            lane = (u * tiles + 2 * supers) * rows
            extra = incoming_ref[own, :, lane : lane + rows].reshape(side, rows).astype(F32)
            for kind in range(2):
                base = (u * tiles + kind * supers) * rows
                last = base + (supers - 1) * rows
                full = incoming_ref[own, :, last : last + rows].reshape(side, rows)
                rest = extra if kind == 0 else roll(extra, rows // 2)
                rest = jnp.where(low, rest, 0.0).astype(BF16)
                near, far = (full, rest) if u else (rest, full)
                for p, diagonal, lane in ((c, near, base), (supers - 1 - c, far, base + c * rows)):
                    slots = slice(p * group + u * side, p * group + (u + 1) * side)
                    if p:
                        dense_ref[kind, slots, : p * rows] = incoming_ref[
                            own, :, lane : lane + p * rows
                        ].reshape(side, p * rows)
                    dense_ref[kind, slots, p * rows : (p + 1) * rows] = diagonal
                    to = (p // CHUNK + 1) * CHUNK * rows
                    if to > (p + 1) * rows:
                        dense_ref[kind, slots, (p + 1) * rows : to] = jnp.zeros(
                            (side, to - (p + 1) * rows), BF16
                        )
    gather = to_slots(supers, 2 * per)
    for kind in range(2):
        columns = slice(kind * width, (kind + 1) * width)
        for j in range(supers // CHUNK):
            first = j * CHUNK
            cut = slice(first * rows, (first + CHUNK) * rows)
            dense = dense_ref[kind, first * group :, cut]
            terms = dot(dense, spread_ref[first * group :, columns], 0, 0).astype(BF16)
            for b in range(CHUNK * SPLIT):
                out_ref[order_ref[first * SPLIT + b], :part, columns] = terms[
                    b * part : (b + 1) * part, :
                ]
            added = dot(dense, key_value_ref[cut, columns])
            if j == 0:
                sum_ref[...] = added
            else:
                sum_ref[first * group :, :] = sum_ref[first * group :, :] + added
        found = jnp.where(own_head(sum_ref.shape), sum_ref[...], 0.0).astype(BF16)
        lines = dot(gather, found, 0, 0).astype(BF16)
        for p in range(blocks):
            out_ref[order_ref[p], part:, columns] = lines[p * strip : (p + 1) * strip, :]


def final_kernel(
    received_ref, attended_ref, query_ref, key_ref, value_ref, keys_ref, lines_ref,
    *, blocks, rows, strip, width
):
    part = rows // SPLIT
    for k in range(SPLIT):
        total = received_ref[k, :part, :].astype(F32)
        for s in range(k + SPLIT, blocks, SPLIT):
            total += received_ref[s, :part, :].astype(F32)
        keys_ref[k * part : (k + 1) * part, :] = total.astype(BF16)
    for n in range(blocks // SPLIT):
        total = received_ref[n * SPLIT, part:, :].astype(F32)
        for k in range(1, SPLIT):
            total += received_ref[n * SPLIT + k, part:, :].astype(F32)
        lines_ref[n * strip : (n + 1) * strip, :] = total
    lines = dot(to_classes(rows, blocks // SPLIT), lines_ref[...].astype(BF16), 0, 0).astype(BF16)
    keys = dot(to_classes(rows, SPLIT), keys_ref[...], 0, 0).astype(BF16)
    query_ref[...] = lines[:, :width]
    attended_ref[...] = lines[:, width:]
    key_ref[...] = keys[:, :width]
    value_ref[...] = keys[:, width:]


def body(query_rows, key_rows, value_rows, out_grad, mix_pre, mix_post, block_order):
    blocks = lax.axis_size("seq")
    owners = lax.axis_size("row") * lax.axis_size("col")
    rows, width = query_rows.shape
    heads = mix_pre.shape[0]
    scaling = DH ** (-0.5)
    strip = rows // blocks * SPLIT
    supers = blocks // SPLIT
    span = 2 * (supers + 1) * rows
    keys = supers * rows
    lines = blocks * strip
    slots = lines * HEADS
    whole = pl.BlockSpec(memory_space=pltpu.VMEM)
    table = pl.BlockSpec(memory_space=pltpu.SMEM)
    seq_shape = (blocks, rows // SPLIT + strip, 2 * width)
    head_shape = (owners, HEADS, 2 * (2 * supers + 1) * rows)
    static = dict(blocks=blocks, rows=rows, strip=strip)

    def call(kernel, ins, outs, scratch=(), dtype=BF16, **more):
        return pl.pallas_call(
            functools.partial(kernel, **static, **more),
            in_specs=ins,
            out_specs=[whole] * len(outs),
            out_shape=[jax.ShapeDtypeStruct(shape, dtype) for shape in outs],
            scratch_shapes=scratch,
            compiler_params=pltpu.CompilerParams(vmem_limit_bytes=VMEM_LIMIT),
            interpret=INTERP,
        )

    def exchange(values, axes):
        return near(lax.all_to_all(values, axes, split_axis=0, concat_axis=0, tiled=True))

    def near(values):
        return values if INTERP else pltpu.with_memory_space_constraint(values, pltpu.VMEM)

    def far(values):
        return values if INTERP else pltpu.with_memory_space_constraint(values, pltpu.HBM)

    (sent,) = call(
        send_kernel,
        [pl.BlockSpec(memory_space=pltpu.HBM)] * 4,
        [seq_shape],
        [pltpu.VMEM((rows, width), BF16)] * 4 + [pltpu.SemaphoreType.DMA((4,))],
        width=width,
    )(*[far(values) for values in (query_rows, key_rows, value_rows, out_grad)])
    received = exchange(sent, "seq")
    sorted_blocks = [
        pltpu.SMEM((blocks,), jnp.int32),
        pltpu.VMEM((keys, 2 * width), BF16),
        pltpu.VMEM((slots, 2 * width), BF16),
        pltpu.VMEM((lines, 2 * width), F32),
    ]
    (packed,) = call(
        score_kernel,
        [table, whole],
        [head_shape],
        sorted_blocks + [pltpu.VMEM((2, supers, HEADS * strip * SPLIT, rows), F32)],
        width=width, scaling=scaling,
    )(block_order, received)
    weights, squashed, grads, sums = call(
        weigh_kernel,
        [whole] * 3,
        [(heads, span)] * 3 + [(heads, rows)],
        dtype=F32, heads=heads,
    )(exchange(packed, HEAD_AXES), mix_pre, mix_post)
    others = lax.ppermute(sums, "seq", [(s, s ^ 1) for s in range(blocks)])
    (mixed,) = call(
        mix_kernel,
        [whole] * 7,
        [head_shape],
        [pltpu.VMEM((2, heads, span), BF16)],
        heads=heads, scaling=scaling,
    )(near(weights), near(squashed), near(grads), sums, near(others), mix_pre, mix_post)
    (sent,) = call(
        grad_kernel,
        [table, whole, whole],
        [seq_shape],
        [pltpu.VMEM((2, slots, keys), BF16), pltpu.VMEM((slots, width), F32)] + sorted_blocks,
        width=width,
    )(block_order, exchange(mixed, HEAD_AXES), received)
    return call(
        final_kernel,
        [whole],
        [(rows, width)] * 4,
        [pltpu.VMEM((rows, 2 * width), BF16), pltpu.VMEM((rows, 2 * width), F32)],
        width=width,
    )(exchange(sent, "seq"))


def solution(mesh):
    spread = P("seq", HEAD_AXES)
    return jax.shard_map(
        body,
        mesh=mesh,
        in_specs=(spread, spread, spread, spread, P(), P(), P()),
        out_specs=(spread, spread, spread, spread),
        check_vma=False,
    )
```

```python
import functools

import jax
import jax.numpy as jnp
from jax import lax
from jax.experimental import pallas as pl
from jax.experimental.pallas import tpu as pltpu
from jax.sharding import PartitionSpec as P

DH = 128


logit_cap = 10.0

HEAD_AXES = ("row", "col")
HEADS = 2
CHUNK = 2
SPLIT = 2
VMEM_LIMIT = 24 << 20
INTERP = False
BF16, F32 = jnp.bfloat16, jnp.float32


def dot(left, right, left_dim=1, right_dim=0):
    return lax.dot_general(
        left, right, (((left_dim,), (right_dim,)), ((), ())), preferred_element_type=F32
    )


def iota(shape, dim):
    return lax.broadcasted_iota(jnp.int32, shape, dim)


def to_classes(rows, classes):
    row, column = iota((rows, rows), 0), iota((rows, rows), 1)
    per = rows // classes
    return jnp.where(row % per * classes + row // per == column, 1.0, 0.0).astype(BF16)


def to_slots(supers, reach):
    shape = (supers * reach * HEADS, supers * reach)
    row, column = iota(shape, 0), iota(shape, 1)
    block, slot = row // (reach * HEADS), row // HEADS % reach
    line = jnp.where(block < supers // 2, slot, reach - 1 - slot)
    return jnp.where(block * reach + line == column, 1.0, 0.0).astype(BF16)


def own_head(shape):
    return iota(shape, 0) % HEADS == iota(shape, 1) // DH % HEADS


def send_kernel(
    query_hbm, key_hbm, value_hbm, grad_hbm, out_ref, query_ref, key_ref, value_ref, grad_ref, sems,
    *, blocks, rows, strip, width
):
    copies = [
        pltpu.make_async_copy(source, target, sems.at[n])
        for n, (source, target) in enumerate(
            [
                (query_hbm, query_ref),
                (grad_hbm, grad_ref),
                (key_hbm, key_ref),
                (value_hbm, value_ref),
            ]
        )
    ]
    for copy in copies:
        copy.start()
    pick_keys, pick_lines = to_classes(rows, SPLIT), to_classes(rows, blocks // SPLIT)
    for copy in copies:
        copy.wait()
    queries = dot(pick_lines, query_ref[...]).astype(BF16)
    grads = dot(pick_lines, grad_ref[...]).astype(BF16)
    keys = dot(pick_keys, key_ref[...]).astype(BF16)
    values = dot(pick_keys, value_ref[...]).astype(BF16)
    part = rows // SPLIT
    for s in range(blocks):
        key_cut = slice(s % SPLIT * part, (s % SPLIT + 1) * part)
        line_cut = slice(s // SPLIT * strip, (s // SPLIT + 1) * strip)
        out_ref[s, :part, :width] = keys[key_cut, :]
        out_ref[s, :part, width:] = values[key_cut, :]
        out_ref[s, part:, :width] = queries[line_cut, :]
        out_ref[s, part:, width:] = grads[line_cut, :]


def sort_blocks(
    block_ref, received_ref, order_ref, key_value_ref, spread_ref, lines_ref, blocks, rows, strip
):
    part = rows // SPLIT
    for s in range(blocks):
        order_ref[block_ref[s]] = s
    for p in range(blocks):
        source = order_ref[p]
        key_value_ref[p * part : (p + 1) * part, :] = received_ref[source, :part, :]
        lines_ref[p * strip : (p + 1) * strip, :] = received_ref[source, part:, :].astype(F32)
    spread = dot(to_slots(blocks // SPLIT, strip * SPLIT), lines_ref[...].astype(BF16))
    spread_ref[...] = jnp.where(own_head(spread.shape), spread, 0.0).astype(BF16)


def score_kernel(
    block_ref, received_ref, out_ref, order_ref, key_value_ref, spread_ref, lines_ref, diagonal_ref,
    *, blocks, rows, strip, width, scaling
):
    supers = blocks // SPLIT
    half = supers // 2
    per = strip * SPLIT // 2
    side = per * HEADS
    group = 2 * side
    sort_blocks(
        block_ref, received_ref, order_ref, key_value_ref, spread_ref, lines_ref, blocks, rows, strip
    )
    for kind in range(2):
        columns = slice(kind * width, (kind + 1) * width)
        for j in range(supers // CHUNK):
            first = j * CHUNK
            scores = dot(
                spread_ref[first * group :, columns],
                key_value_ref[first * rows : (first + CHUNK) * rows, columns],
                1,
                1,
            )
            if kind == 0:
                scores = scores * scaling
            for p in range(first, supers):
                piece = scores[(p - first) * group : (p - first + 1) * group, :]
                count = min(p - first, CHUNK)
                if p - first < CHUNK:
                    diagonal_ref[kind, p] = piece[:, count * rows : (count + 1) * rows]
                if count:
                    c = min(p, supers - 1 - p)
                    skip = kind * supers + (first if p < half else supers - 1 - p + first)
                    for u in range(2):
                        lane = (2 * u * supers + skip) * rows
                        out_ref[c * per : (c + 1) * per, :, lane : lane + count * rows] = (
                            piece[u * side : (u + 1) * side, : count * rows]
                            .astype(BF16)
                            .reshape(per, HEADS, count * rows)
                        )
    lane_of = iota((side, rows), 1)
    for c in range(half):
        cut = slice(c * per, (c + 1) * per)
        shared = jnp.zeros((side, rows), F32)
        for u in range(2):
            own = slice(u * side, (u + 1) * side)
            taken = blended(side, rows, u)
            for kind in range(2):
                near = diagonal_ref[kind, c, own]
                far = diagonal_ref[kind, supers - 1 - c, own]
                late, early = (near, far) if u else (far, near)
                full = jnp.where(taken, roll(early, rows // 2), late)
                lane = (2 * u * supers + (kind + 1) * supers - 1) * rows
                out_ref[cut, :, lane : lane + rows] = full.astype(BF16).reshape(per, HEADS, rows)
                quarter = 2 * u + kind
                shared = jnp.where(
                    lane_of // (rows // 4) == quarter, roll(early, quarter * rows // 4), shared
                )
        out_ref[cut, :, 4 * supers * rows :] = shared.astype(BF16).reshape(per, HEADS, rows)


def blended(side, rows, u):
    late_slot = iota((side, rows), 0) >= side // 2
    return (iota((side, rows), 1) >= rows * 3 // 4) & (late_slot if u == 0 else ~late_slot)


def roll(values, shift):
    shift %= values.shape[1]
    if shift == 0:
        return values
    if INTERP:
        return jnp.roll(values, shift, 1)
    return pltpu.roll(values, shift, 1)


def near_tiles(pair, supers, u):
    return [j < pair for j in range(supers - 1)] + [u == 1, u == 0]


def early_lanes(lane, slot, per, u):
    start = lane.shape[1] * 3 // 4
    blend = slot >= per // 2 if u == 0 else slot < per // 2
    return lane >= jnp.where(blend, start, lane.shape[1])


def weigh_kernel(
    incoming_ref, pre_ref, post_ref, weight_ref, squashed_ref, grad_ref, sum_ref,
    *, blocks, rows, strip, heads
):
    supers = blocks // SPLIT
    per = strip * SPLIT // 2
    own = lax.axis_index(HEAD_AXES)
    pair, slot = lax.div(own, per), lax.rem(own, per)
    seq = lax.axis_index("seq")
    line_class, key_class = lax.div(seq, SPLIT), lax.rem(seq, SPLIT)
    pre, post = pre_ref[...], post_ref[...]
    lane = iota((heads, rows), 1)
    full = supers * rows
    sums = jnp.zeros((heads, rows), F32)
    shared = incoming_ref[:, :, 4 * full :].reshape(heads, rows)
    shared_mixed, shared_grads = dot(pre, shared), dot(post, shared, 0, 0)
    for u in range(2):
        base = 2 * u * full
        mine = u * (supers + 1) * rows
        squashed_ref[:, mine : mine + full] = dot(
            pre, incoming_ref[:, :, base : base + full].reshape(heads, full)
        )
        squashed_ref[:, mine + full : mine + full + rows] = roll(
            shared_mixed, -2 * u * (rows // 4)
        )
        grad_ref[:, mine : mine + full] = dot(
            post, incoming_ref[:, :, base + full : base + 2 * full].reshape(heads, full), 0, 0
        )
        grad_ref[:, mine + full : mine + full + rows] = roll(
            shared_grads, -(2 * u + 1) * (rows // 4)
        )
        line = slot + u * per
        limits = []
        for at in (line, 2 * per - 1 - line):
            offset = at * (blocks // SPLIT) + line_class
            limits.append(lax.div(offset - key_class + SPLIT, SPLIT) - 1)
        late_limit, early_limit = limits if u else limits[::-1]
        taken = early_lanes(lane, slot, per, u)
        is_near = near_tiles(pair, supers, u)
        zero = jnp.zeros((heads, rows), F32)
        parts = [zero, zero, zero, zero]
        for j in range(supers + 1):
            cut = slice(mine + j * rows, mine + (j + 1) * rows)
            squashed = jnp.tanh(squashed_ref[:, cut] / logit_cap)
            weights = jnp.exp(logit_cap * squashed)
            if j == supers - 1:
                limit = jnp.where(taken, early_limit + rows // 2, late_limit)
                weights = jnp.where(lane <= limit, weights, 0.0)
            elif j == supers:
                limit = jnp.minimum(early_limit, rows // 4 - 1)
                weights = jnp.where(lane <= limit, weights, 0.0)
            squashed_ref[:, cut] = squashed
            weight_ref[:, cut] = weights
            dots = weights * grad_ref[:, cut]
            near = jnp.where(is_near[j], 1.0, 0.0)
            if j == supers - 1:
                near = jnp.where(taken, 1.0 - near, near)
            for n, values in enumerate((weights, dots)):
                parts[2 * n] += values * near
                parts[2 * n + 1] += values * (1.0 - near)
        for n, values in enumerate(parts):
            down = jnp.sum(values, axis=1, keepdims=True)
            sums += jnp.where(lane == 4 * u + n, down, 0.0)
    sum_ref[...] = sums


def mix_kernel(
    weight_ref, squashed_ref, grad_ref, own_ref, other_ref, pre_ref, post_ref, out_ref, both_ref,
    *, blocks, rows, strip, heads, scaling
):
    supers = blocks // SPLIT
    per = strip * SPLIT // 2
    own = lax.axis_index(HEAD_AXES)
    pair, slot = lax.div(own, per), lax.rem(own, per)
    owners = heads // HEADS
    full = supers * rows
    pre, post = pre_ref[...], post_ref[...]
    lane = iota((heads, rows), 1)
    sums = own_ref[...] + other_ref[...]
    shared = jnp.zeros((heads, rows), F32)
    for u in range(2):
        base = 2 * u * full
        mine = u * (supers + 1) * rows
        near_total, far_total, near_dot, far_dot = [
            jnp.sum(jnp.where(lane == 4 * u + n, sums, 0.0), axis=1, keepdims=True)
            for n in range(4)
        ]
        near_scale, far_scale = 1.0 / near_total, 1.0 / far_total
        near_row, far_row = near_dot * near_scale, far_dot * far_scale
        is_near = near_tiles(pair, supers, u)
        for j in range(supers + 1):
            cut = slice(mine + j * rows, mine + (j + 1) * rows)
            here = is_near[j]
            if j == supers - 1:
                here = early_lanes(lane, slot, per, u) ^ (u == 1)
            probs = weight_ref[:, cut] * jnp.where(here, near_scale, far_scale)
            squashed = squashed_ref[:, cut]
            grad_capped = probs * (grad_ref[:, cut] - jnp.where(here, near_row, far_row))
            both_ref[0, :, cut] = (grad_capped * (1.0 - squashed * squashed)).astype(BF16)
            both_ref[1, :, cut] = probs.astype(BF16)
        cut = slice(mine, mine + full + rows)
        grad_scores = dot(pre, both_ref[0, :, cut], 0, 0) * scaling
        post_mixed = dot(post, both_ref[1, :, cut])
        for kind, values in enumerate((grad_scores, post_mixed)):
            quarter = 2 * u + kind
            shared = jnp.where(
                lane // (rows // 4) == quarter,
                roll(values[:, full:], quarter * rows // 4),
                shared,
            )
        shape = (owners, HEADS, full)
        out_ref[:, :, base : base + full] = grad_scores[:, :full].astype(BF16).reshape(shape)
        out_ref[:, :, base + full : base + 2 * full] = (
            post_mixed[:, :full].astype(BF16).reshape(shape)
        )
    out_ref[:, :, 4 * full :] = shared.astype(BF16).reshape(owners, HEADS, rows)


def grad_kernel(
    block_ref, incoming_ref, received_ref, out_ref, dense_ref, sum_ref, order_ref, key_value_ref,
    spread_ref, lines_ref, *, blocks, rows, strip, width
):
    supers = blocks // SPLIT
    half = supers // 2
    per = strip * SPLIT // 2
    side = per * HEADS
    group = 2 * side
    part = rows // SPLIT
    sort_blocks(
        block_ref, received_ref, order_ref, key_value_ref, spread_ref, lines_ref, blocks, rows, strip
    )
    lane_of = iota((side, rows), 1)
    for c in range(half):
        own = slice(c * per, (c + 1) * per)
        shared = incoming_ref[own, :, 4 * supers * rows :].reshape(side, rows).astype(F32)
        for u in range(2):
            taken = blended(side, rows, u)
            for kind in range(2):
                base = (2 * u + kind) * supers * rows
                last = base + (supers - 1) * rows
                full = incoming_ref[own, :, last : last + rows].reshape(side, rows).astype(F32)
                late = jnp.where(taken, 0.0, full).astype(BF16)
                second = roll(jnp.where(taken, full, 0.0), rows // 2)
                first = roll(shared, -(2 * u + kind) * (rows // 4))
                early = jnp.where(lane_of < rows // 4, first, second).astype(BF16)
                near, far = (late, early) if u else (early, late)
                for p, diagonal, lane in ((c, near, base), (supers - 1 - c, far, base + c * rows)):
                    slots = slice(p * group + u * side, p * group + (u + 1) * side)
                    if p:
                        dense_ref[kind, slots, : p * rows] = incoming_ref[
                            own, :, lane : lane + p * rows
                        ].reshape(side, p * rows)
                    dense_ref[kind, slots, p * rows : (p + 1) * rows] = diagonal
                    to = (p // CHUNK + 1) * CHUNK * rows
                    if to > (p + 1) * rows:
                        dense_ref[kind, slots, (p + 1) * rows : to] = jnp.zeros(
                            (side, to - (p + 1) * rows), BF16
                        )
    gather = to_slots(supers, 2 * per)
    for kind in range(2):
        columns = slice(kind * width, (kind + 1) * width)
        for j in range(supers // CHUNK):
            first = j * CHUNK
            cut = slice(first * rows, (first + CHUNK) * rows)
            dense = dense_ref[kind, first * group :, cut]
            terms = dot(dense, spread_ref[first * group :, columns], 0, 0).astype(BF16)
            for b in range(CHUNK * SPLIT):
                out_ref[order_ref[first * SPLIT + b], :part, columns] = terms[
                    b * part : (b + 1) * part, :
                ]
            added = dot(dense, key_value_ref[cut, columns])
            if j == 0:
                sum_ref[...] = added
            else:
                sum_ref[first * group :, :] = sum_ref[first * group :, :] + added
        found = jnp.where(own_head(sum_ref.shape), sum_ref[...], 0.0).astype(BF16)
        lines = dot(gather, found, 0, 0).astype(BF16)
        for p in range(blocks):
            out_ref[order_ref[p], part:, columns] = lines[p * strip : (p + 1) * strip, :]


def final_kernel(
    received_ref, attended_ref, query_ref, key_ref, value_ref, keys_ref, lines_ref,
    *, blocks, rows, strip, width
):
    part = rows // SPLIT
    for k in range(SPLIT):
        total = received_ref[k, :part, :].astype(F32)
        for s in range(k + SPLIT, blocks, SPLIT):
            total += received_ref[s, :part, :].astype(F32)
        keys_ref[k * part : (k + 1) * part, :] = total.astype(BF16)
    for n in range(blocks // SPLIT):
        total = received_ref[n * SPLIT, part:, :].astype(F32)
        for k in range(1, SPLIT):
            total += received_ref[n * SPLIT + k, part:, :].astype(F32)
        lines_ref[n * strip : (n + 1) * strip, :] = total
    lines = dot(to_classes(rows, blocks // SPLIT), lines_ref[...].astype(BF16), 0, 0).astype(BF16)
    keys = dot(to_classes(rows, SPLIT), keys_ref[...], 0, 0).astype(BF16)
    query_ref[...] = lines[:, :width]
    attended_ref[...] = lines[:, width:]
    key_ref[...] = keys[:, :width]
    value_ref[...] = keys[:, width:]


def body(query_rows, key_rows, value_rows, out_grad, mix_pre, mix_post, block_order):
    blocks = lax.axis_size("seq")
    owners = lax.axis_size("row") * lax.axis_size("col")
    rows, width = query_rows.shape
    heads = mix_pre.shape[0]
    scaling = DH ** (-0.5)
    strip = rows // blocks * SPLIT
    supers = blocks // SPLIT
    span = 2 * (supers + 1) * rows
    keys = supers * rows
    lines = blocks * strip
    slots = lines * HEADS
    whole = pl.BlockSpec(memory_space=pltpu.VMEM)
    table = pl.BlockSpec(memory_space=pltpu.SMEM)
    seq_shape = (blocks, rows // SPLIT + strip, 2 * width)
    head_shape = (owners, HEADS, (4 * supers + 1) * rows)
    static = dict(blocks=blocks, rows=rows, strip=strip)

    def call(kernel, ins, outs, scratch=(), dtype=BF16, **more):
        return pl.pallas_call(
            functools.partial(kernel, **static, **more),
            in_specs=ins,
            out_specs=[whole] * len(outs),
            out_shape=[jax.ShapeDtypeStruct(shape, dtype) for shape in outs],
            scratch_shapes=scratch,
            compiler_params=pltpu.CompilerParams(vmem_limit_bytes=VMEM_LIMIT),
            interpret=INTERP,
        )

    def exchange(values, axes):
        return near(lax.all_to_all(values, axes, split_axis=0, concat_axis=0, tiled=True))

    def near(values):
        return values if INTERP else pltpu.with_memory_space_constraint(values, pltpu.VMEM)

    def far(values):
        return values if INTERP else pltpu.with_memory_space_constraint(values, pltpu.HBM)

    (sent,) = call(
        send_kernel,
        [pl.BlockSpec(memory_space=pltpu.HBM)] * 4,
        [seq_shape],
        [pltpu.VMEM((rows, width), BF16)] * 4 + [pltpu.SemaphoreType.DMA((4,))],
        width=width,
    )(*[far(values) for values in (query_rows, key_rows, value_rows, out_grad)])
    received = exchange(sent, "seq")
    sorted_blocks = [
        pltpu.SMEM((blocks,), jnp.int32),
        pltpu.VMEM((keys, 2 * width), BF16),
        pltpu.VMEM((slots, 2 * width), BF16),
        pltpu.VMEM((lines, 2 * width), F32),
    ]
    (packed,) = call(
        score_kernel,
        [table, whole],
        [head_shape],
        sorted_blocks + [pltpu.VMEM((2, supers, HEADS * strip * SPLIT, rows), F32)],
        width=width, scaling=scaling,
    )(block_order, received)
    weights, squashed, grads, sums = call(
        weigh_kernel,
        [whole] * 3,
        [(heads, span)] * 3 + [(heads, rows)],
        dtype=F32, heads=heads,
    )(exchange(packed, HEAD_AXES), mix_pre, mix_post)
    others = lax.ppermute(sums, "seq", [(s, s ^ 1) for s in range(blocks)])
    (mixed,) = call(
        mix_kernel,
        [whole] * 7,
        [head_shape],
        [pltpu.VMEM((2, heads, span), BF16)],
        heads=heads, scaling=scaling,
    )(near(weights), near(squashed), near(grads), sums, near(others), mix_pre, mix_post)
    (sent,) = call(
        grad_kernel,
        [table, whole, whole],
        [seq_shape],
        [pltpu.VMEM((2, slots, keys), BF16), pltpu.VMEM((slots, width), F32)] + sorted_blocks,
        width=width,
    )(block_order, exchange(mixed, HEAD_AXES), received)
    return call(
        final_kernel,
        [whole],
        [(rows, width)] * 4,
        [pltpu.VMEM((rows, 2 * width), BF16), pltpu.VMEM((rows, 2 * width), F32)],
        width=width,
    )(exchange(sent, "seq"))


def solution(mesh):
    spread = P("seq", HEAD_AXES)
    return jax.shard_map(
        body,
        mesh=mesh,
        in_specs=(spread, spread, spread, spread, P(), P(), P()),
        out_specs=(spread, spread, spread, spread),
        check_vma=False,
    )
```

```python
import functools

import jax
import jax.numpy as jnp
from jax import lax
from jax.experimental import pallas as pl
from jax.experimental.pallas import tpu as pltpu
from jax.sharding import PartitionSpec as P

DH = 128


logit_cap = 10.0

HEAD_AXES = ("row", "col")
HEADS = 2
CHUNK = 2
SPLIT = 2
SUMS = 8
VMEM_LIMIT = 24 << 20
INTERP = False
BF16, F32 = jnp.bfloat16, jnp.float32


def dot(left, right, left_dim=1, right_dim=0):
    return lax.dot_general(
        left, right, (((left_dim,), (right_dim,)), ((), ())), preferred_element_type=F32
    )


def iota(shape, dim):
    return lax.broadcasted_iota(jnp.int32, shape, dim)


def to_classes(rows, classes):
    row, column = iota((rows, rows), 0), iota((rows, rows), 1)
    per = rows // classes
    return jnp.where(row % per * classes + row // per == column, 1.0, 0.0).astype(BF16)


def to_slots(supers, reach):
    shape = (supers * reach * HEADS, supers * reach)
    row, column = iota(shape, 0), iota(shape, 1)
    block, slot = row // (reach * HEADS), row // HEADS % reach
    line = jnp.where(block < supers // 2, slot, reach - 1 - slot)
    return jnp.where(block * reach + line == column, 1.0, 0.0).astype(BF16)


def own_head(shape):
    return iota(shape, 0) % HEADS == iota(shape, 1) // DH % HEADS


def send_kernel(
    query_hbm, key_hbm, value_hbm, grad_hbm, out_ref, query_ref, key_ref, value_ref, grad_ref, sems,
    *, blocks, rows, strip, width
):
    copies = [
        pltpu.make_async_copy(source, target, sems.at[n])
        for n, (source, target) in enumerate(
            [
                (query_hbm, query_ref),
                (grad_hbm, grad_ref),
                (key_hbm, key_ref),
                (value_hbm, value_ref),
            ]
        )
    ]
    for copy in copies:
        copy.start()
    pick_keys, pick_lines = to_classes(rows, SPLIT), to_classes(rows, blocks // SPLIT)
    for copy in copies:
        copy.wait()
    queries = dot(pick_lines, query_ref[...]).astype(BF16)
    grads = dot(pick_lines, grad_ref[...]).astype(BF16)
    keys = dot(pick_keys, key_ref[...]).astype(BF16)
    values = dot(pick_keys, value_ref[...]).astype(BF16)
    part = rows // SPLIT
    for s in range(blocks):
        key_cut = slice(s % SPLIT * part, (s % SPLIT + 1) * part)
        line_cut = slice(s // SPLIT * strip, (s // SPLIT + 1) * strip)
        out_ref[s, :part, :width] = keys[key_cut, :]
        out_ref[s, :part, width:] = values[key_cut, :]
        out_ref[s, part:, :width] = queries[line_cut, :]
        out_ref[s, part:, width:] = grads[line_cut, :]


def sort_blocks(
    block_ref, received_ref, order_ref, key_value_ref, spread_ref, lines_ref, blocks, rows, strip
):
    part = rows // SPLIT
    for s in range(blocks):
        order_ref[block_ref[s]] = s
    for p in range(blocks):
        source = order_ref[p]
        key_value_ref[p * part : (p + 1) * part, :] = received_ref[source, :part, :]
        lines_ref[p * strip : (p + 1) * strip, :] = received_ref[source, part:, :].astype(F32)
    spread = dot(to_slots(blocks // SPLIT, strip * SPLIT), lines_ref[...].astype(BF16))
    spread_ref[...] = jnp.where(own_head(spread.shape), spread, 0.0).astype(BF16)


def score_kernel(
    block_ref, received_ref, out_ref, key_value_ref, spread_ref, order_ref, lines_ref, diagonal_ref,
    *, blocks, rows, strip, width, scaling
):
    supers = blocks // SPLIT
    half = supers // 2
    per = strip * SPLIT // 2
    side = per * HEADS
    group = 2 * side
    sort_blocks(
        block_ref, received_ref, order_ref, key_value_ref, spread_ref, lines_ref, blocks, rows, strip
    )
    for kind in range(2):
        columns = slice(kind * width, (kind + 1) * width)
        for j in range(supers // CHUNK):
            first = j * CHUNK
            scores = dot(
                spread_ref[first * group :, columns],
                key_value_ref[first * rows : (first + CHUNK) * rows, columns],
                1,
                1,
            )
            if kind == 0:
                scores = scores * scaling
            for p in range(first, supers):
                piece = scores[(p - first) * group : (p - first + 1) * group, :]
                count = min(p - first, CHUNK)
                if p - first < CHUNK:
                    diagonal_ref[kind, p] = piece[:, count * rows : (count + 1) * rows]
                if count:
                    c = min(p, supers - 1 - p)
                    skip = kind * supers + (first if p < half else supers - 1 - p + first)
                    for u in range(2):
                        lane = (2 * u * supers + skip) * rows
                        out_ref[c * per : (c + 1) * per, :, lane : lane + count * rows] = (
                            piece[u * side : (u + 1) * side, : count * rows]
                            .astype(BF16)
                            .reshape(per, HEADS, count * rows)
                        )
    lane_of = iota((side, rows), 1)
    for c in range(half):
        cut = slice(c * per, (c + 1) * per)
        shared = jnp.zeros((side, rows), F32)
        for u in range(2):
            own = slice(u * side, (u + 1) * side)
            taken = blended(side, rows, u)
            for kind in range(2):
                near = diagonal_ref[kind, c, own]
                far = diagonal_ref[kind, supers - 1 - c, own]
                late, early = (near, far) if u else (far, near)
                full = jnp.where(taken, roll(early, rows // 2), late)
                lane = (2 * u * supers + (kind + 1) * supers - 1) * rows
                out_ref[cut, :, lane : lane + rows] = full.astype(BF16).reshape(per, HEADS, rows)
                quarter = 2 * u + kind
                shared = jnp.where(
                    lane_of // (rows // 4) == quarter, roll(early, quarter * rows // 4), shared
                )
        out_ref[cut, :, 4 * supers * rows :] = shared.astype(BF16).reshape(per, HEADS, rows)


def blended(side, rows, u):
    late_slot = iota((side, rows), 0) >= side // 2
    return (iota((side, rows), 1) >= rows * 3 // 4) & (late_slot if u == 0 else ~late_slot)


def roll(values, shift):
    shift %= values.shape[1]
    if shift == 0:
        return values
    if INTERP:
        return jnp.roll(values, shift, 1)
    return pltpu.roll(values, shift, 1)


def near_tiles(pair, supers, u):
    return [j < pair for j in range(supers - 1)] + [u == 1, u == 0]


def early_lanes(lane, slot, per, u):
    start = lane.shape[1] * 3 // 4
    blend = slot >= per // 2 if u == 0 else slot < per // 2
    return lane >= jnp.where(blend, start, lane.shape[1])


def weigh_kernel(
    incoming_ref, pre_ref, post_ref, weight_ref, squashed_ref, grad_ref, sum_ref,
    *, blocks, rows, strip, heads
):
    supers = blocks // SPLIT
    per = strip * SPLIT // 2
    own = lax.axis_index(HEAD_AXES)
    pair, slot = lax.div(own, per), lax.rem(own, per)
    seq = lax.axis_index("seq")
    line_class, key_class = lax.div(seq, SPLIT), lax.rem(seq, SPLIT)
    pre, post = pre_ref[...], post_ref[...]
    lane = iota((heads, rows), 1)
    full = supers * rows
    sums = jnp.zeros((heads, rows), F32)
    shared = incoming_ref[:, :, 4 * full :].reshape(heads, rows)
    shared_mixed, shared_grads = dot(pre, shared), dot(post, shared, 0, 0)
    for u in range(2):
        base = 2 * u * full
        mine = u * (supers + 1) * rows
        squashed_ref[:, mine : mine + full] = dot(
            pre, incoming_ref[:, :, base : base + full].reshape(heads, full)
        )
        squashed_ref[:, mine + full : mine + full + rows] = roll(
            shared_mixed, -2 * u * (rows // 4)
        )
        grad_ref[:, mine : mine + full] = dot(
            post, incoming_ref[:, :, base + full : base + 2 * full].reshape(heads, full), 0, 0
        )
        grad_ref[:, mine + full : mine + full + rows] = roll(
            shared_grads, -(2 * u + 1) * (rows // 4)
        )
        line = slot + u * per
        limits = []
        for at in (line, 2 * per - 1 - line):
            offset = at * (blocks // SPLIT) + line_class
            limits.append(lax.div(offset - key_class + SPLIT, SPLIT) - 1)
        late_limit, early_limit = limits if u else limits[::-1]
        taken = early_lanes(lane, slot, per, u)
        is_near = near_tiles(pair, supers, u)
        zero = jnp.zeros((heads, rows), F32)
        parts = [zero, zero, zero, zero]
        for j in range(supers + 1):
            cut = slice(mine + j * rows, mine + (j + 1) * rows)
            squashed = jnp.tanh(squashed_ref[:, cut] / logit_cap)
            weights = jnp.exp(logit_cap * squashed)
            if j == supers - 1:
                limit = jnp.where(taken, early_limit + rows // 2, late_limit)
                weights = jnp.where(lane <= limit, weights, 0.0)
            elif j == supers:
                limit = jnp.minimum(early_limit, rows // 4 - 1)
                weights = jnp.where(lane <= limit, weights, 0.0)
            squashed_ref[:, cut] = squashed
            weight_ref[:, cut] = weights
            dots = weights * grad_ref[:, cut]
            near = jnp.where(is_near[j], 1.0, 0.0)
            if j == supers - 1:
                near = jnp.where(taken, 1.0 - near, near)
            for n, values in enumerate((weights, dots)):
                parts[2 * n] += values * near
                parts[2 * n + 1] += values * (1.0 - near)
        for n, values in enumerate(parts):
            down = jnp.sum(values, axis=1, keepdims=True)
            sums += jnp.where(lane == 4 * u + n, down, 0.0)
    sum_ref[...] = jnp.transpose(sums)[:SUMS]


def mix_kernel(
    weight_ref, squashed_ref, grad_ref, own_ref, other_ref, pre_ref, post_ref, out_ref, both_ref,
    *, blocks, rows, strip, heads, scaling
):
    supers = blocks // SPLIT
    per = strip * SPLIT // 2
    own = lax.axis_index(HEAD_AXES)
    pair, slot = lax.div(own, per), lax.rem(own, per)
    owners = heads // HEADS
    full = supers * rows
    pre, post = pre_ref[...], post_ref[...]
    lane = iota((heads, rows), 1)
    sums = own_ref[...] + other_ref[...]
    if rows > SUMS:
        sums = jnp.concatenate([sums, jnp.zeros((rows - SUMS, heads), F32)], axis=0)
    sums = jnp.transpose(sums)
    shared = jnp.zeros((heads, rows), F32)
    for u in range(2):
        base = 2 * u * full
        mine = u * (supers + 1) * rows
        near_total, far_total, near_dot, far_dot = [
            jnp.sum(jnp.where(lane == 4 * u + n, sums, 0.0), axis=1, keepdims=True)
            for n in range(4)
        ]
        near_scale, far_scale = 1.0 / near_total, 1.0 / far_total
        near_row, far_row = near_dot * near_scale, far_dot * far_scale
        is_near = near_tiles(pair, supers, u)
        for j in range(supers + 1):
            cut = slice(mine + j * rows, mine + (j + 1) * rows)
            here = is_near[j]
            if j == supers - 1:
                here = early_lanes(lane, slot, per, u) ^ (u == 1)
            probs = weight_ref[:, cut] * jnp.where(here, near_scale, far_scale)
            squashed = squashed_ref[:, cut]
            grad_capped = probs * (grad_ref[:, cut] - jnp.where(here, near_row, far_row))
            both_ref[0, :, cut] = (grad_capped * (1.0 - squashed * squashed)).astype(BF16)
            both_ref[1, :, cut] = probs.astype(BF16)
        cut = slice(mine, mine + full + rows)
        grad_scores = dot(pre, both_ref[0, :, cut], 0, 0) * scaling
        post_mixed = dot(post, both_ref[1, :, cut])
        for kind, values in enumerate((grad_scores, post_mixed)):
            quarter = 2 * u + kind
            shared = jnp.where(
                lane // (rows // 4) == quarter,
                roll(values[:, full:], quarter * rows // 4),
                shared,
            )
        shape = (owners, HEADS, full)
        out_ref[:, :, base : base + full] = grad_scores[:, :full].astype(BF16).reshape(shape)
        out_ref[:, :, base + full : base + 2 * full] = (
            post_mixed[:, :full].astype(BF16).reshape(shape)
        )
    out_ref[:, :, 4 * full :] = shared.astype(BF16).reshape(owners, HEADS, rows)


def grad_kernel(
    block_ref, incoming_ref, key_value_ref, spread_ref, out_ref, dense_ref, sum_ref, order_ref,
    *, blocks, rows, strip, width
):
    supers = blocks // SPLIT
    half = supers // 2
    per = strip * SPLIT // 2
    side = per * HEADS
    group = 2 * side
    part = rows // SPLIT
    for s in range(blocks):
        order_ref[block_ref[s]] = s
    lane_of = iota((side, rows), 1)
    for c in range(half):
        own = slice(c * per, (c + 1) * per)
        shared = incoming_ref[own, :, 4 * supers * rows :].reshape(side, rows).astype(F32)
        for u in range(2):
            taken = blended(side, rows, u)
            for kind in range(2):
                base = (2 * u + kind) * supers * rows
                last = base + (supers - 1) * rows
                full = incoming_ref[own, :, last : last + rows].reshape(side, rows).astype(F32)
                late = jnp.where(taken, 0.0, full).astype(BF16)
                second = roll(jnp.where(taken, full, 0.0), rows // 2)
                first = roll(shared, -(2 * u + kind) * (rows // 4))
                early = jnp.where(lane_of < rows // 4, first, second).astype(BF16)
                near, far = (late, early) if u else (early, late)
                for p, diagonal, lane in ((c, near, base), (supers - 1 - c, far, base + c * rows)):
                    slots = slice(p * group + u * side, p * group + (u + 1) * side)
                    if p:
                        dense_ref[kind, slots, : p * rows] = incoming_ref[
                            own, :, lane : lane + p * rows
                        ].reshape(side, p * rows)
                    dense_ref[kind, slots, p * rows : (p + 1) * rows] = diagonal
                    to = (p // CHUNK + 1) * CHUNK * rows
                    if to > (p + 1) * rows:
                        dense_ref[kind, slots, (p + 1) * rows : to] = jnp.zeros(
                            (side, to - (p + 1) * rows), BF16
                        )
    gather = to_slots(supers, 2 * per)
    for kind in range(2):
        columns = slice(kind * width, (kind + 1) * width)
        for j in range(supers // CHUNK):
            first = j * CHUNK
            cut = slice(first * rows, (first + CHUNK) * rows)
            dense = dense_ref[kind, first * group :, cut]
            terms = dot(dense, spread_ref[first * group :, columns], 0, 0).astype(BF16)
            for b in range(CHUNK * SPLIT):
                out_ref[order_ref[first * SPLIT + b], :part, columns] = terms[
                    b * part : (b + 1) * part, :
                ]
            added = dot(dense, key_value_ref[cut, columns])
            if j == 0:
                sum_ref[...] = added
            else:
                sum_ref[first * group :, :] = sum_ref[first * group :, :] + added
        found = jnp.where(own_head(sum_ref.shape), sum_ref[...], 0.0).astype(BF16)
        lines = dot(gather, found, 0, 0).astype(BF16)
        for p in range(blocks):
            out_ref[order_ref[p], part:, columns] = lines[p * strip : (p + 1) * strip, :]


def final_kernel(
    received_ref, attended_ref, query_ref, key_ref, value_ref, keys_ref, lines_ref,
    *, blocks, rows, strip, width
):
    part = rows // SPLIT
    for k in range(SPLIT):
        total = received_ref[k, :part, :].astype(F32)
        for s in range(k + SPLIT, blocks, SPLIT):
            total += received_ref[s, :part, :].astype(F32)
        keys_ref[k * part : (k + 1) * part, :] = total.astype(BF16)
    for n in range(blocks // SPLIT):
        total = received_ref[n * SPLIT, part:, :].astype(F32)
        for k in range(1, SPLIT):
            total += received_ref[n * SPLIT + k, part:, :].astype(F32)
        lines_ref[n * strip : (n + 1) * strip, :] = total
    lines = dot(to_classes(rows, blocks // SPLIT), lines_ref[...].astype(BF16), 0, 0).astype(BF16)
    keys = dot(to_classes(rows, SPLIT), keys_ref[...], 0, 0).astype(BF16)
    query_ref[...] = lines[:, :width]
    attended_ref[...] = lines[:, width:]
    key_ref[...] = keys[:, :width]
    value_ref[...] = keys[:, width:]


def body(query_rows, key_rows, value_rows, out_grad, mix_pre, mix_post, block_order):
    blocks = lax.axis_size("seq")
    owners = lax.axis_size("row") * lax.axis_size("col")
    rows, width = query_rows.shape
    heads = mix_pre.shape[0]
    scaling = DH ** (-0.5)
    strip = rows // blocks * SPLIT
    supers = blocks // SPLIT
    span = 2 * (supers + 1) * rows
    keys = supers * rows
    lines = blocks * strip
    slots = lines * HEADS
    whole = pl.BlockSpec(memory_space=pltpu.VMEM)
    table = pl.BlockSpec(memory_space=pltpu.SMEM)
    seq_shape = (blocks, rows // SPLIT + strip, 2 * width)
    head_shape = (owners, HEADS, (4 * supers + 1) * rows)
    static = dict(blocks=blocks, rows=rows, strip=strip)

    def call(kernel, ins, outs, scratch=(), dtype=BF16, **more):
        return pl.pallas_call(
            functools.partial(kernel, **static, **more),
            in_specs=ins,
            out_specs=[whole] * len(outs),
            out_shape=[jax.ShapeDtypeStruct(shape, dtype) for shape in outs],
            scratch_shapes=scratch,
            compiler_params=pltpu.CompilerParams(vmem_limit_bytes=VMEM_LIMIT),
            interpret=INTERP,
        )

    def exchange(values, axes):
        return near(lax.all_to_all(values, axes, split_axis=0, concat_axis=0, tiled=True))

    def near(values):
        return values if INTERP else pltpu.with_memory_space_constraint(values, pltpu.VMEM)

    def far(values):
        return values if INTERP else pltpu.with_memory_space_constraint(values, pltpu.HBM)

    (sent,) = call(
        send_kernel,
        [pl.BlockSpec(memory_space=pltpu.HBM)] * 4,
        [seq_shape],
        [pltpu.VMEM((rows, width), BF16)] * 4 + [pltpu.SemaphoreType.DMA((4,))],
        width=width,
    )(*[far(values) for values in (query_rows, key_rows, value_rows, out_grad)])
    received = exchange(sent, "seq")
    packed, key_value, line_rows = call(
        score_kernel,
        [table, whole],
        [head_shape, (keys, 2 * width), (slots, 2 * width)],
        [
            pltpu.SMEM((blocks,), jnp.int32),
            pltpu.VMEM((lines, 2 * width), F32),
            pltpu.VMEM((2, supers, HEADS * strip * SPLIT, rows), F32),
        ],
        width=width, scaling=scaling,
    )(block_order, received)
    weights, squashed, grads, sums = call(
        weigh_kernel,
        [whole] * 3,
        [(heads, span)] * 3 + [(SUMS, heads)],
        dtype=F32, heads=heads,
    )(exchange(packed, HEAD_AXES), mix_pre, mix_post)
    others = lax.ppermute(sums, "seq", [(s, s ^ 1) for s in range(blocks)])
    (mixed,) = call(
        mix_kernel,
        [whole] * 7,
        [head_shape],
        [pltpu.VMEM((2, heads, span), BF16)],
        heads=heads, scaling=scaling,
    )(near(weights), near(squashed), near(grads), sums, near(others), mix_pre, mix_post)
    (sent,) = call(
        grad_kernel,
        [table, whole, whole, whole],
        [seq_shape],
        [
            pltpu.VMEM((2, slots, keys), BF16),
            pltpu.VMEM((slots, width), F32),
            pltpu.SMEM((blocks,), jnp.int32),
        ],
        width=width,
    )(block_order, exchange(mixed, HEAD_AXES), near(key_value), near(line_rows))
    return call(
        final_kernel,
        [whole],
        [(rows, width)] * 4,
        [pltpu.VMEM((rows, 2 * width), BF16), pltpu.VMEM((rows, 2 * width), F32)],
        width=width,
    )(exchange(sent, "seq"))


def solution(mesh):
    spread = P("seq", HEAD_AXES)
    return jax.shard_map(
        body,
        mesh=mesh,
        in_specs=(spread, spread, spread, spread, P(), P(), P()),
        out_specs=(spread, spread, spread, spread),
        check_vma=False,
    )
```

```python
import functools

import jax
import jax.numpy as jnp
from jax import lax
from jax.experimental import pallas as pl
from jax.experimental.pallas import tpu as pltpu
from jax.sharding import PartitionSpec as P

DH = 128


logit_cap = 10.0

HEAD_AXES = ("row", "col")
OWNER_AXES = ("col", "row")
HEADS = 2
CHUNK = 2
SPLIT = 2
SUMS = 8
VMEM_LIMIT = 24 << 20
INTERP = False
BF16, F32 = jnp.bfloat16, jnp.float32


def dot(left, right, left_dim=1, right_dim=0):
    return lax.dot_general(
        left, right, (((left_dim,), (right_dim,)), ((), ())), preferred_element_type=F32
    )


def iota(shape, dim):
    return lax.broadcasted_iota(jnp.int32, shape, dim)


def to_classes(rows, classes):
    row, column = iota((rows, rows), 0), iota((rows, rows), 1)
    per = rows // classes
    return jnp.where(row % per * classes + row // per == column, 1.0, 0.0).astype(BF16)


def to_slots(supers, reach):
    shape = (supers * reach * HEADS, supers * reach)
    row, column = iota(shape, 0), iota(shape, 1)
    block, slot = row // (reach * HEADS), row // HEADS % reach
    line = jnp.where(block < supers // 2, slot, reach - 1 - slot)
    return jnp.where(block * reach + line == column, 1.0, 0.0).astype(BF16)


def exchange_order(pre_ref, post_ref, heads, outer):
    row, column = iota((heads, heads), 0), iota((heads, heads), 1)
    owner = row // HEADS
    inner = heads // HEADS // outer
    stored = (owner % outer * inner + owner // outer) * HEADS + row % HEADS
    pick = jnp.where(stored == column, 1.0, 0.0).astype(BF16)
    return dot(pre_ref[...], pick, 1, 1).astype(BF16), dot(pick, post_ref[...]).astype(BF16)


def own_head(shape):
    return iota(shape, 0) % HEADS == iota(shape, 1) // DH % HEADS


def send_kernel(
    query_hbm, key_hbm, value_hbm, grad_hbm, out_ref, query_ref, key_ref, value_ref, grad_ref, sems,
    *, blocks, rows, strip, width
):
    copies = [
        pltpu.make_async_copy(source, target, sems.at[n])
        for n, (source, target) in enumerate(
            [
                (query_hbm, query_ref),
                (grad_hbm, grad_ref),
                (key_hbm, key_ref),
                (value_hbm, value_ref),
            ]
        )
    ]
    for copy in copies:
        copy.start()
    pick_keys, pick_lines = to_classes(rows, SPLIT), to_classes(rows, blocks // SPLIT)
    for copy in copies:
        copy.wait()
    queries = dot(pick_lines, query_ref[...]).astype(BF16)
    grads = dot(pick_lines, grad_ref[...]).astype(BF16)
    keys = dot(pick_keys, key_ref[...]).astype(BF16)
    values = dot(pick_keys, value_ref[...]).astype(BF16)
    part = rows // SPLIT
    for s in range(blocks):
        key_cut = slice(s % SPLIT * part, (s % SPLIT + 1) * part)
        line_cut = slice(s // SPLIT * strip, (s // SPLIT + 1) * strip)
        out_ref[s, :part, :width] = keys[key_cut, :]
        out_ref[s, :part, width:] = values[key_cut, :]
        out_ref[s, part:, :width] = queries[line_cut, :]
        out_ref[s, part:, width:] = grads[line_cut, :]


def sort_blocks(
    block_ref, received_ref, order_ref, key_value_ref, spread_ref, lines_ref, blocks, rows, strip
):
    part = rows // SPLIT
    for s in range(blocks):
        order_ref[block_ref[s]] = s
    for p in range(blocks):
        source = order_ref[p]
        key_value_ref[p * part : (p + 1) * part, :] = received_ref[source, :part, :]
        lines_ref[p * strip : (p + 1) * strip, :] = received_ref[source, part:, :].astype(F32)
    spread = dot(to_slots(blocks // SPLIT, strip * SPLIT), lines_ref[...].astype(BF16))
    spread_ref[...] = jnp.where(own_head(spread.shape), spread, 0.0).astype(BF16)


def score_kernel(
    block_ref, received_ref, out_ref, key_value_ref, spread_ref, order_ref, lines_ref, diagonal_ref,
    *, blocks, rows, strip, width, scaling
):
    supers = blocks // SPLIT
    half = supers // 2
    per = strip * SPLIT // 2
    side = per * HEADS
    group = 2 * side
    sort_blocks(
        block_ref, received_ref, order_ref, key_value_ref, spread_ref, lines_ref, blocks, rows, strip
    )
    for kind in range(2):
        columns = slice(kind * width, (kind + 1) * width)
        for j in range(supers // CHUNK):
            first = j * CHUNK
            scores = dot(
                spread_ref[first * group :, columns],
                key_value_ref[first * rows : (first + CHUNK) * rows, columns],
                1,
                1,
            )
            if kind == 0:
                scores = scores * scaling
            for p in range(first, supers):
                piece = scores[(p - first) * group : (p - first + 1) * group, :]
                count = min(p - first, CHUNK)
                if p - first < CHUNK:
                    diagonal_ref[kind, p] = piece[:, count * rows : (count + 1) * rows]
                if count:
                    c = min(p, supers - 1 - p)
                    skip = kind * supers + (first if p < half else supers - 1 - p + first)
                    for u in range(2):
                        lane = (2 * u * supers + skip) * rows
                        out_ref[c * per : (c + 1) * per, :, lane : lane + count * rows] = (
                            piece[u * side : (u + 1) * side, : count * rows]
                            .astype(BF16)
                            .reshape(per, HEADS, count * rows)
                        )
    lane_of = iota((side, rows), 1)
    for c in range(half):
        cut = slice(c * per, (c + 1) * per)
        shared = jnp.zeros((side, rows), F32)
        for u in range(2):
            own = slice(u * side, (u + 1) * side)
            taken = blended(side, rows, u)
            for kind in range(2):
                near = diagonal_ref[kind, c, own]
                far = diagonal_ref[kind, supers - 1 - c, own]
                late, early = (near, far) if u else (far, near)
                full = jnp.where(taken, roll(early, rows // 2), late)
                lane = (2 * u * supers + (kind + 1) * supers - 1) * rows
                out_ref[cut, :, lane : lane + rows] = full.astype(BF16).reshape(per, HEADS, rows)
                quarter = 2 * u + kind
                shared = jnp.where(
                    lane_of // (rows // 4) == quarter, roll(early, quarter * rows // 4), shared
                )
        out_ref[cut, :, 4 * supers * rows :] = shared.astype(BF16).reshape(per, HEADS, rows)


def blended(side, rows, u):
    late_slot = iota((side, rows), 0) >= side // 2
    return (iota((side, rows), 1) >= rows * 3 // 4) & (late_slot if u == 0 else ~late_slot)


def roll(values, shift):
    shift %= values.shape[1]
    if shift == 0:
        return values
    if INTERP:
        return jnp.roll(values, shift, 1)
    return pltpu.roll(values, shift, 1)


def near_tiles(pair, supers, u):
    return [j < pair for j in range(supers - 1)] + [u == 1, u == 0]


def early_lanes(lane, slot, per, u):
    start = lane.shape[1] * 3 // 4
    blend = slot >= per // 2 if u == 0 else slot < per // 2
    return lane >= jnp.where(blend, start, lane.shape[1])


def weigh_kernel(
    incoming_ref, pre_ref, post_ref, weight_ref, squashed_ref, grad_ref, sum_ref,
    *, blocks, rows, strip, heads, outer
):
    supers = blocks // SPLIT
    per = strip * SPLIT // 2
    own = lax.axis_index(OWNER_AXES)
    pair, slot = lax.div(own, per), lax.rem(own, per)
    seq = lax.axis_index("seq")
    line_class, key_class = lax.div(seq, SPLIT), lax.rem(seq, SPLIT)
    pre, post = exchange_order(pre_ref, post_ref, heads, outer)
    lane = iota((heads, rows), 1)
    full = supers * rows
    sums = jnp.zeros((heads, rows), F32)
    shared = incoming_ref[:, :, 4 * full :].reshape(heads, rows)
    shared_mixed, shared_grads = dot(pre, shared), dot(post, shared, 0, 0)
    for u in range(2):
        base = 2 * u * full
        mine = u * (supers + 1) * rows
        squashed_ref[:, mine : mine + full] = dot(
            pre, incoming_ref[:, :, base : base + full].reshape(heads, full)
        )
        squashed_ref[:, mine + full : mine + full + rows] = roll(
            shared_mixed, -2 * u * (rows // 4)
        )
        grad_ref[:, mine : mine + full] = dot(
            post, incoming_ref[:, :, base + full : base + 2 * full].reshape(heads, full), 0, 0
        )
        grad_ref[:, mine + full : mine + full + rows] = roll(
            shared_grads, -(2 * u + 1) * (rows // 4)
        )
        line = slot + u * per
        limits = []
        for at in (line, 2 * per - 1 - line):
            offset = at * (blocks // SPLIT) + line_class
            limits.append(lax.div(offset - key_class + SPLIT, SPLIT) - 1)
        late_limit, early_limit = limits if u else limits[::-1]
        taken = early_lanes(lane, slot, per, u)
        is_near = near_tiles(pair, supers, u)
        zero = jnp.zeros((heads, rows), F32)
        parts = [zero, zero, zero, zero]
        for j in range(supers + 1):
            cut = slice(mine + j * rows, mine + (j + 1) * rows)
            squashed = jnp.tanh(squashed_ref[:, cut] / logit_cap)
            weights = jnp.exp(logit_cap * squashed)
            if j == supers - 1:
                limit = jnp.where(taken, early_limit + rows // 2, late_limit)
                weights = jnp.where(lane <= limit, weights, 0.0)
            elif j == supers:
                limit = jnp.minimum(early_limit, rows // 4 - 1)
                weights = jnp.where(lane <= limit, weights, 0.0)
            squashed_ref[:, cut] = squashed
            weight_ref[:, cut] = weights
            dots = weights * grad_ref[:, cut]
            near = jnp.where(is_near[j], 1.0, 0.0)
            if j == supers - 1:
                near = jnp.where(taken, 1.0 - near, near)
            for n, values in enumerate((weights, dots)):
                parts[2 * n] += values * near
                parts[2 * n + 1] += values * (1.0 - near)
        for n, values in enumerate(parts):
            down = jnp.sum(values, axis=1, keepdims=True)
            sums += jnp.where(lane == 4 * u + n, down, 0.0)
    sum_ref[...] = jnp.transpose(sums)[:SUMS]


def mix_kernel(
    weight_ref, squashed_ref, grad_ref, own_ref, other_ref, pre_ref, post_ref, out_ref, both_ref,
    *, blocks, rows, strip, heads, outer, scaling
):
    supers = blocks // SPLIT
    per = strip * SPLIT // 2
    own = lax.axis_index(OWNER_AXES)
    pair, slot = lax.div(own, per), lax.rem(own, per)
    owners = heads // HEADS
    full = supers * rows
    pre, post = exchange_order(pre_ref, post_ref, heads, outer)
    lane = iota((heads, rows), 1)
    sums = own_ref[...] + other_ref[...]
    if rows > SUMS:
        sums = jnp.concatenate([sums, jnp.zeros((rows - SUMS, heads), F32)], axis=0)
    sums = jnp.transpose(sums)
    shared = jnp.zeros((heads, rows), F32)
    for u in range(2):
        base = 2 * u * full
        mine = u * (supers + 1) * rows
        near_total, far_total, near_dot, far_dot = [
            jnp.sum(jnp.where(lane == 4 * u + n, sums, 0.0), axis=1, keepdims=True)
            for n in range(4)
        ]
        near_scale, far_scale = 1.0 / near_total, 1.0 / far_total
        near_row, far_row = near_dot * near_scale, far_dot * far_scale
        is_near = near_tiles(pair, supers, u)
        for j in range(supers + 1):
            cut = slice(mine + j * rows, mine + (j + 1) * rows)
            here = is_near[j]
            if j == supers - 1:
                here = early_lanes(lane, slot, per, u) ^ (u == 1)
            probs = weight_ref[:, cut] * jnp.where(here, near_scale, far_scale)
            squashed = squashed_ref[:, cut]
            grad_capped = probs * (grad_ref[:, cut] - jnp.where(here, near_row, far_row))
            both_ref[0, :, cut] = (grad_capped * (1.0 - squashed * squashed)).astype(BF16)
            both_ref[1, :, cut] = probs.astype(BF16)
        cut = slice(mine, mine + full + rows)
        grad_scores = dot(pre, both_ref[0, :, cut], 0, 0) * scaling
        post_mixed = dot(post, both_ref[1, :, cut])
        for kind, values in enumerate((grad_scores, post_mixed)):
            quarter = 2 * u + kind
            shared = jnp.where(
                lane // (rows // 4) == quarter,
                roll(values[:, full:], quarter * rows // 4),
                shared,
            )
        shape = (owners, HEADS, full)
        out_ref[:, :, base : base + full] = grad_scores[:, :full].astype(BF16).reshape(shape)
        out_ref[:, :, base + full : base + 2 * full] = (
            post_mixed[:, :full].astype(BF16).reshape(shape)
        )
    out_ref[:, :, 4 * full :] = shared.astype(BF16).reshape(owners, HEADS, rows)


def grad_kernel(
    block_ref, incoming_ref, key_value_ref, spread_ref, out_ref, dense_ref, sum_ref, order_ref,
    *, blocks, rows, strip, width
):
    supers = blocks // SPLIT
    half = supers // 2
    per = strip * SPLIT // 2
    side = per * HEADS
    group = 2 * side
    part = rows // SPLIT
    for s in range(blocks):
        order_ref[block_ref[s]] = s
    lane_of = iota((side, rows), 1)
    for c in range(half):
        own = slice(c * per, (c + 1) * per)
        shared = incoming_ref[own, :, 4 * supers * rows :].reshape(side, rows).astype(F32)
        for u in range(2):
            taken = blended(side, rows, u)
            for kind in range(2):
                base = (2 * u + kind) * supers * rows
                last = base + (supers - 1) * rows
                full = incoming_ref[own, :, last : last + rows].reshape(side, rows).astype(F32)
                late = jnp.where(taken, 0.0, full).astype(BF16)
                second = roll(jnp.where(taken, full, 0.0), rows // 2)
                first = roll(shared, -(2 * u + kind) * (rows // 4))
                early = jnp.where(lane_of < rows // 4, first, second).astype(BF16)
                near, far = (late, early) if u else (early, late)
                for p, diagonal, lane in ((c, near, base), (supers - 1 - c, far, base + c * rows)):
                    slots = slice(p * group + u * side, p * group + (u + 1) * side)
                    if p:
                        dense_ref[kind, slots, : p * rows] = incoming_ref[
                            own, :, lane : lane + p * rows
                        ].reshape(side, p * rows)
                    dense_ref[kind, slots, p * rows : (p + 1) * rows] = diagonal
                    to = (p // CHUNK + 1) * CHUNK * rows
                    if to > (p + 1) * rows:
                        dense_ref[kind, slots, (p + 1) * rows : to] = jnp.zeros(
                            (side, to - (p + 1) * rows), BF16
                        )
    gather = to_slots(supers, 2 * per)
    for kind in range(2):
        columns = slice(kind * width, (kind + 1) * width)
        for j in range(supers // CHUNK):
            first = j * CHUNK
            cut = slice(first * rows, (first + CHUNK) * rows)
            dense = dense_ref[kind, first * group :, cut]
            terms = dot(dense, spread_ref[first * group :, columns], 0, 0).astype(BF16)
            for b in range(CHUNK * SPLIT):
                out_ref[order_ref[first * SPLIT + b], :part, columns] = terms[
                    b * part : (b + 1) * part, :
                ]
            added = dot(dense, key_value_ref[cut, columns])
            if j == 0:
                sum_ref[...] = added
            else:
                sum_ref[first * group :, :] = sum_ref[first * group :, :] + added
        found = jnp.where(own_head(sum_ref.shape), sum_ref[...], 0.0).astype(BF16)
        lines = dot(gather, found, 0, 0).astype(BF16)
        for p in range(blocks):
            out_ref[order_ref[p], part:, columns] = lines[p * strip : (p + 1) * strip, :]


def final_kernel(
    received_ref, attended_ref, query_ref, key_ref, value_ref, keys_ref, lines_ref,
    *, blocks, rows, strip, width
):
    part = rows // SPLIT
    for k in range(SPLIT):
        total = received_ref[k, :part, :].astype(F32)
        for s in range(k + SPLIT, blocks, SPLIT):
            total += received_ref[s, :part, :].astype(F32)
        keys_ref[k * part : (k + 1) * part, :] = total.astype(BF16)
    for n in range(blocks // SPLIT):
        total = received_ref[n * SPLIT, part:, :].astype(F32)
        for k in range(1, SPLIT):
            total += received_ref[n * SPLIT + k, part:, :].astype(F32)
        lines_ref[n * strip : (n + 1) * strip, :] = total
    lines = dot(to_classes(rows, blocks // SPLIT), lines_ref[...].astype(BF16), 0, 0).astype(BF16)
    keys = dot(to_classes(rows, SPLIT), keys_ref[...], 0, 0).astype(BF16)
    query_ref[...] = lines[:, :width]
    attended_ref[...] = lines[:, width:]
    key_ref[...] = keys[:, :width]
    value_ref[...] = keys[:, width:]


def body(query_rows, key_rows, value_rows, out_grad, mix_pre, mix_post, block_order):
    blocks = lax.axis_size("seq")
    outer = lax.axis_size("row")
    owners = outer * lax.axis_size("col")
    rows, width = query_rows.shape
    heads = mix_pre.shape[0]
    scaling = DH ** (-0.5)
    strip = rows // blocks * SPLIT
    supers = blocks // SPLIT
    span = 2 * (supers + 1) * rows
    keys = supers * rows
    lines = blocks * strip
    slots = lines * HEADS
    whole = pl.BlockSpec(memory_space=pltpu.VMEM)
    table = pl.BlockSpec(memory_space=pltpu.SMEM)
    seq_shape = (blocks, rows // SPLIT + strip, 2 * width)
    head_shape = (owners, HEADS, (4 * supers + 1) * rows)
    static = dict(blocks=blocks, rows=rows, strip=strip)

    def call(kernel, ins, outs, scratch=(), dtype=BF16, **more):
        return pl.pallas_call(
            functools.partial(kernel, **static, **more),
            in_specs=ins,
            out_specs=[whole] * len(outs),
            out_shape=[jax.ShapeDtypeStruct(shape, dtype) for shape in outs],
            scratch_shapes=scratch,
            compiler_params=pltpu.CompilerParams(vmem_limit_bytes=VMEM_LIMIT),
            interpret=INTERP,
        )

    def exchange(values, axes):
        return near(lax.all_to_all(values, axes, split_axis=0, concat_axis=0, tiled=True))

    def near(values):
        return values if INTERP else pltpu.with_memory_space_constraint(values, pltpu.VMEM)

    def far(values):
        return values if INTERP else pltpu.with_memory_space_constraint(values, pltpu.HBM)

    (sent,) = call(
        send_kernel,
        [pl.BlockSpec(memory_space=pltpu.HBM)] * 4,
        [seq_shape],
        [pltpu.VMEM((rows, width), BF16)] * 4 + [pltpu.SemaphoreType.DMA((4,))],
        width=width,
    )(*[far(values) for values in (query_rows, key_rows, value_rows, out_grad)])
    received = exchange(sent, "seq")
    packed, key_value, line_rows = call(
        score_kernel,
        [table, whole],
        [head_shape, (keys, 2 * width), (slots, 2 * width)],
        [
            pltpu.SMEM((blocks,), jnp.int32),
            pltpu.VMEM((lines, 2 * width), F32),
            pltpu.VMEM((2, supers, HEADS * strip * SPLIT, rows), F32),
        ],
        width=width, scaling=scaling,
    )(block_order, received)
    weights, squashed, grads, sums = call(
        weigh_kernel,
        [whole] * 3,
        [(heads, span)] * 3 + [(SUMS, heads)],
        dtype=F32, heads=heads, outer=outer,
    )(exchange(packed, OWNER_AXES), mix_pre, mix_post)
    others = lax.ppermute(sums, "seq", [(s, s ^ 1) for s in range(blocks)])
    (mixed,) = call(
        mix_kernel,
        [whole] * 7,
        [head_shape],
        [pltpu.VMEM((2, heads, span), BF16)],
        heads=heads, outer=outer, scaling=scaling,
    )(near(weights), near(squashed), near(grads), sums, near(others), mix_pre, mix_post)
    (sent,) = call(
        grad_kernel,
        [table, whole, whole, whole],
        [seq_shape],
        [
            pltpu.VMEM((2, slots, keys), BF16),
            pltpu.VMEM((slots, width), F32),
            pltpu.SMEM((blocks,), jnp.int32),
        ],
        width=width,
    )(block_order, exchange(mixed, OWNER_AXES), near(key_value), near(line_rows))
    return call(
        final_kernel,
        [whole],
        [(rows, width)] * 4,
        [pltpu.VMEM((rows, 2 * width), BF16), pltpu.VMEM((rows, 2 * width), F32)],
        width=width,
    )(exchange(sent, "seq"))


def solution(mesh):
    spread = P("seq", HEAD_AXES)
    return jax.shard_map(
        body,
        mesh=mesh,
        in_specs=(spread, spread, spread, spread, P(), P(), P()),
        out_specs=(spread, spread, spread, spread),
        check_vma=False,
    )
```

```python
import functools

import jax
import jax.numpy as jnp
from jax import lax
from jax.experimental import pallas as pl
from jax.experimental.pallas import tpu as pltpu
from jax.sharding import PartitionSpec as P

DH = 128


logit_cap = 10.0

HEAD_AXES = ("row", "col")
OWNER_AXES = ("col", "row")
HEADS = 2
CHUNK = 4
SPLIT = 2
SUMS = 8
VMEM_LIMIT = 24 << 20
INTERP = False
BF16, F32 = jnp.bfloat16, jnp.float32


def dot(left, right, left_dim=1, right_dim=0):
    return lax.dot_general(
        left, right, (((left_dim,), (right_dim,)), ((), ())), preferred_element_type=F32
    )


def iota(shape, dim):
    return lax.broadcasted_iota(jnp.int32, shape, dim)


def to_classes(rows, classes):
    row, column = iota((rows, rows), 0), iota((rows, rows), 1)
    per = rows // classes
    return jnp.where(row % per * classes + row // per == column, 1.0, 0.0).astype(BF16)


def to_slots(supers, reach):
    shape = (supers * reach * HEADS, supers * reach)
    row, column = iota(shape, 0), iota(shape, 1)
    block, slot = row // (reach * HEADS), row // HEADS % reach
    line = jnp.where(block < supers // 2, slot, reach - 1 - slot)
    return jnp.where(block * reach + line == column, 1.0, 0.0).astype(BF16)


def exchange_order(pre_ref, post_ref, heads, outer):
    row, column = iota((heads, heads), 0), iota((heads, heads), 1)
    owner = row // HEADS
    inner = heads // HEADS // outer
    stored = (owner % outer * inner + owner // outer) * HEADS + row % HEADS
    pick = jnp.where(stored == column, 1.0, 0.0).astype(BF16)
    return dot(pre_ref[...], pick, 1, 1).astype(BF16), dot(pick, post_ref[...]).astype(BF16)


def own_head(shape):
    return iota(shape, 0) % HEADS == iota(shape, 1) // DH % HEADS


def send_kernel(
    query_hbm, key_hbm, value_hbm, grad_hbm, out_ref, query_ref, key_ref, value_ref, grad_ref, sems,
    *, blocks, rows, strip, width
):
    copies = [
        pltpu.make_async_copy(source, target, sems.at[n])
        for n, (source, target) in enumerate(
            [
                (query_hbm, query_ref),
                (grad_hbm, grad_ref),
                (key_hbm, key_ref),
                (value_hbm, value_ref),
            ]
        )
    ]
    for copy in copies:
        copy.start()
    pick_keys, pick_lines = to_classes(rows, SPLIT), to_classes(rows, blocks // SPLIT)
    for copy in copies:
        copy.wait()
    queries = dot(pick_lines, query_ref[...]).astype(BF16)
    grads = dot(pick_lines, grad_ref[...]).astype(BF16)
    keys = dot(pick_keys, key_ref[...]).astype(BF16)
    values = dot(pick_keys, value_ref[...]).astype(BF16)
    part = rows // SPLIT
    for s in range(blocks):
        key_cut = slice(s % SPLIT * part, (s % SPLIT + 1) * part)
        line_cut = slice(s // SPLIT * strip, (s // SPLIT + 1) * strip)
        out_ref[s, :part, :width] = keys[key_cut, :]
        out_ref[s, :part, width:] = values[key_cut, :]
        out_ref[s, part:, :width] = queries[line_cut, :]
        out_ref[s, part:, width:] = grads[line_cut, :]


def sort_blocks(
    block_ref, received_ref, order_ref, key_value_ref, spread_ref, lines_ref, blocks, rows, strip
):
    part = rows // SPLIT
    for s in range(blocks):
        order_ref[block_ref[s]] = s
    for p in range(blocks):
        source = order_ref[p]
        key_value_ref[p * part : (p + 1) * part, :] = received_ref[source, :part, :]
        lines_ref[p * strip : (p + 1) * strip, :] = received_ref[source, part:, :].astype(F32)
    spread = dot(to_slots(blocks // SPLIT, strip * SPLIT), lines_ref[...].astype(BF16))
    spread_ref[...] = jnp.where(own_head(spread.shape), spread, 0.0).astype(BF16)


def score_kernel(
    block_ref, received_ref, out_ref, key_value_ref, spread_ref, order_ref, lines_ref, diagonal_ref,
    *, blocks, rows, strip, width, scaling
):
    supers = blocks // SPLIT
    half = supers // 2
    per = strip * SPLIT // 2
    side = per * HEADS
    group = 2 * side
    sort_blocks(
        block_ref, received_ref, order_ref, key_value_ref, spread_ref, lines_ref, blocks, rows, strip
    )
    for kind in range(2):
        columns = slice(kind * width, (kind + 1) * width)
        for j in range(supers // CHUNK):
            first = j * CHUNK
            scores = dot(
                spread_ref[first * group :, columns],
                key_value_ref[first * rows : (first + CHUNK) * rows, columns],
                1,
                1,
            )
            if kind == 0:
                scores = scores * scaling
            for p in range(first, supers):
                piece = scores[(p - first) * group : (p - first + 1) * group, :]
                count = min(p - first, CHUNK)
                if p - first < CHUNK:
                    diagonal_ref[kind, p] = piece[:, count * rows : (count + 1) * rows]
                if count:
                    c = min(p, supers - 1 - p)
                    skip = kind * supers + (first if p < half else supers - 1 - p + first)
                    for u in range(2):
                        lane = (2 * u * supers + skip) * rows
                        out_ref[c * per : (c + 1) * per, :, lane : lane + count * rows] = (
                            piece[u * side : (u + 1) * side, : count * rows]
                            .astype(BF16)
                            .reshape(per, HEADS, count * rows)
                        )
    lane_of = iota((side, rows), 1)
    for c in range(half):
        cut = slice(c * per, (c + 1) * per)
        shared = jnp.zeros((side, rows), F32)
        for u in range(2):
            own = slice(u * side, (u + 1) * side)
            taken = blended(side, rows, u)
            for kind in range(2):
                near = diagonal_ref[kind, c, own]
                far = diagonal_ref[kind, supers - 1 - c, own]
                late, early = (near, far) if u else (far, near)
                full = jnp.where(taken, roll(early, rows // 2), late)
                lane = (2 * u * supers + (kind + 1) * supers - 1) * rows
                out_ref[cut, :, lane : lane + rows] = full.astype(BF16).reshape(per, HEADS, rows)
                quarter = 2 * u + kind
                shared = jnp.where(
                    lane_of // (rows // 4) == quarter, roll(early, quarter * rows // 4), shared
                )
        out_ref[cut, :, 4 * supers * rows :] = shared.astype(BF16).reshape(per, HEADS, rows)


def blended(side, rows, u):
    late_slot = iota((side, rows), 0) >= side // 2
    return (iota((side, rows), 1) >= rows * 3 // 4) & (late_slot if u == 0 else ~late_slot)


def roll(values, shift):
    shift %= values.shape[1]
    if shift == 0:
        return values
    if INTERP:
        return jnp.roll(values, shift, 1)
    return pltpu.roll(values, shift, 1)


def near_tiles(pair, supers, u):
    return [j < pair for j in range(supers - 1)] + [u == 1, u == 0]


def early_lanes(lane, slot, per, u):
    start = lane.shape[1] * 3 // 4
    blend = slot >= per // 2 if u == 0 else slot < per // 2
    return lane >= jnp.where(blend, start, lane.shape[1])


def weigh_kernel(
    incoming_ref, pre_ref, post_ref, weight_ref, squashed_ref, grad_ref, sum_ref,
    *, blocks, rows, strip, heads, outer
):
    supers = blocks // SPLIT
    per = strip * SPLIT // 2
    own = lax.axis_index(OWNER_AXES)
    pair, slot = lax.div(own, per), lax.rem(own, per)
    seq = lax.axis_index("seq")
    line_class, key_class = lax.div(seq, SPLIT), lax.rem(seq, SPLIT)
    pre, post = exchange_order(pre_ref, post_ref, heads, outer)
    lane = iota((heads, rows), 1)
    full = supers * rows
    sums = jnp.zeros((heads, rows), F32)
    shared = incoming_ref[:, :, 4 * full :].reshape(heads, rows)
    shared_mixed, shared_grads = dot(pre, shared), dot(post, shared, 0, 0)
    for u in range(2):
        base = 2 * u * full
        mine = u * (supers + 1) * rows
        squashed_ref[:, mine : mine + full] = dot(
            pre, incoming_ref[:, :, base : base + full].reshape(heads, full)
        )
        squashed_ref[:, mine + full : mine + full + rows] = roll(
            shared_mixed, -2 * u * (rows // 4)
        )
        grad_ref[:, mine : mine + full] = dot(
            post, incoming_ref[:, :, base + full : base + 2 * full].reshape(heads, full), 0, 0
        )
        grad_ref[:, mine + full : mine + full + rows] = roll(
            shared_grads, -(2 * u + 1) * (rows // 4)
        )
        line = slot + u * per
        limits = []
        for at in (line, 2 * per - 1 - line):
            offset = at * (blocks // SPLIT) + line_class
            limits.append(lax.div(offset - key_class + SPLIT, SPLIT) - 1)
        late_limit, early_limit = limits if u else limits[::-1]
        taken = early_lanes(lane, slot, per, u)
        is_near = near_tiles(pair, supers, u)
        zero = jnp.zeros((heads, rows), F32)
        parts = [zero, zero, zero, zero]
        for j in range(supers + 1):
            cut = slice(mine + j * rows, mine + (j + 1) * rows)
            squashed = jnp.tanh(squashed_ref[:, cut] / logit_cap)
            weights = jnp.exp(logit_cap * squashed)
            if j == supers - 1:
                limit = jnp.where(taken, early_limit + rows // 2, late_limit)
                weights = jnp.where(lane <= limit, weights, 0.0)
            elif j == supers:
                limit = jnp.minimum(early_limit, rows // 4 - 1)
                weights = jnp.where(lane <= limit, weights, 0.0)
            squashed_ref[:, cut] = squashed
            weight_ref[:, cut] = weights
            dots = weights * grad_ref[:, cut]
            near = jnp.where(is_near[j], 1.0, 0.0)
            if j == supers - 1:
                near = jnp.where(taken, 1.0 - near, near)
            for n, values in enumerate((weights, dots)):
                parts[2 * n] += values * near
                parts[2 * n + 1] += values * (1.0 - near)
        for n, values in enumerate(parts):
            down = jnp.sum(values, axis=1, keepdims=True)
            sums += jnp.where(lane == 4 * u + n, down, 0.0)
    sum_ref[...] = jnp.transpose(sums)[:SUMS]


def mix_kernel(
    weight_ref, squashed_ref, grad_ref, own_ref, other_ref, pre_ref, post_ref, out_ref, both_ref,
    *, blocks, rows, strip, heads, outer, scaling
):
    supers = blocks // SPLIT
    per = strip * SPLIT // 2
    own = lax.axis_index(OWNER_AXES)
    pair, slot = lax.div(own, per), lax.rem(own, per)
    owners = heads // HEADS
    full = supers * rows
    pre, post = exchange_order(pre_ref, post_ref, heads, outer)
    lane = iota((heads, rows), 1)
    sums = own_ref[...] + other_ref[...]
    if rows > SUMS:
        sums = jnp.concatenate([sums, jnp.zeros((rows - SUMS, heads), F32)], axis=0)
    sums = jnp.transpose(sums)
    shared = jnp.zeros((heads, rows), F32)
    for u in range(2):
        base = 2 * u * full
        mine = u * (supers + 1) * rows
        near_total, far_total, near_dot, far_dot = [
            jnp.sum(jnp.where(lane == 4 * u + n, sums, 0.0), axis=1, keepdims=True)
            for n in range(4)
        ]
        near_scale, far_scale = 1.0 / near_total, 1.0 / far_total
        near_row, far_row = near_dot * near_scale, far_dot * far_scale
        is_near = near_tiles(pair, supers, u)
        for j in range(supers + 1):
            cut = slice(mine + j * rows, mine + (j + 1) * rows)
            here = is_near[j]
            if j == supers - 1:
                here = early_lanes(lane, slot, per, u) ^ (u == 1)
            probs = weight_ref[:, cut] * jnp.where(here, near_scale, far_scale)
            squashed = squashed_ref[:, cut]
            grad_capped = probs * (grad_ref[:, cut] - jnp.where(here, near_row, far_row))
            both_ref[0, :, cut] = (grad_capped * (1.0 - squashed * squashed)).astype(BF16)
            both_ref[1, :, cut] = probs.astype(BF16)
        cut = slice(mine, mine + full + rows)
        grad_scores = dot(pre, both_ref[0, :, cut], 0, 0) * scaling
        post_mixed = dot(post, both_ref[1, :, cut])
        for kind, values in enumerate((grad_scores, post_mixed)):
            quarter = 2 * u + kind
            shared = jnp.where(
                lane // (rows // 4) == quarter,
                roll(values[:, full:], quarter * rows // 4),
                shared,
            )
        shape = (owners, HEADS, full)
        out_ref[:, :, base : base + full] = grad_scores[:, :full].astype(BF16).reshape(shape)
        out_ref[:, :, base + full : base + 2 * full] = (
            post_mixed[:, :full].astype(BF16).reshape(shape)
        )
    out_ref[:, :, 4 * full :] = shared.astype(BF16).reshape(owners, HEADS, rows)


def grad_kernel(
    block_ref, incoming_ref, key_value_ref, spread_ref, out_ref, dense_ref, sum_ref, order_ref,
    *, blocks, rows, strip, width
):
    supers = blocks // SPLIT
    half = supers // 2
    per = strip * SPLIT // 2
    side = per * HEADS
    group = 2 * side
    part = rows // SPLIT
    for s in range(blocks):
        order_ref[block_ref[s]] = s
    lane_of = iota((side, rows), 1)
    for c in range(half):
        own = slice(c * per, (c + 1) * per)
        shared = incoming_ref[own, :, 4 * supers * rows :].reshape(side, rows).astype(F32)
        for u in range(2):
            taken = blended(side, rows, u)
            for kind in range(2):
                base = (2 * u + kind) * supers * rows
                last = base + (supers - 1) * rows
                full = incoming_ref[own, :, last : last + rows].reshape(side, rows).astype(F32)
                late = jnp.where(taken, 0.0, full).astype(BF16)
                second = roll(jnp.where(taken, full, 0.0), rows // 2)
                first = roll(shared, -(2 * u + kind) * (rows // 4))
                early = jnp.where(lane_of < rows // 4, first, second).astype(BF16)
                near, far = (late, early) if u else (early, late)
                for p, diagonal, lane in ((c, near, base), (supers - 1 - c, far, base + c * rows)):
                    slots = slice(p * group + u * side, p * group + (u + 1) * side)
                    if p:
                        dense_ref[kind, slots, : p * rows] = incoming_ref[
                            own, :, lane : lane + p * rows
                        ].reshape(side, p * rows)
                    dense_ref[kind, slots, p * rows : (p + 1) * rows] = diagonal
                    to = (p // CHUNK + 1) * CHUNK * rows
                    if to > (p + 1) * rows:
                        dense_ref[kind, slots, (p + 1) * rows : to] = jnp.zeros(
                            (side, to - (p + 1) * rows), BF16
                        )
    gather = to_slots(supers, 2 * per)
    for kind in range(2):
        columns = slice(kind * width, (kind + 1) * width)
        for j in range(supers // CHUNK):
            first = j * CHUNK
            cut = slice(first * rows, (first + CHUNK) * rows)
            dense = dense_ref[kind, first * group :, cut]
            terms = dot(dense, spread_ref[first * group :, columns], 0, 0).astype(BF16)
            for b in range(CHUNK * SPLIT):
                out_ref[order_ref[first * SPLIT + b], :part, columns] = terms[
                    b * part : (b + 1) * part, :
                ]
            added = dot(dense, key_value_ref[cut, columns])
            if j == 0:
                sum_ref[...] = added
            else:
                sum_ref[first * group :, :] = sum_ref[first * group :, :] + added
        found = jnp.where(own_head(sum_ref.shape), sum_ref[...], 0.0).astype(BF16)
        lines = dot(gather, found, 0, 0).astype(BF16)
        for p in range(blocks):
            out_ref[order_ref[p], part:, columns] = lines[p * strip : (p + 1) * strip, :]


def final_kernel(
    received_ref, attended_ref, query_ref, key_ref, value_ref, keys_ref, lines_ref,
    *, blocks, rows, strip, width
):
    part = rows // SPLIT
    for k in range(SPLIT):
        total = received_ref[k, :part, :].astype(F32)
        for s in range(k + SPLIT, blocks, SPLIT):
            total += received_ref[s, :part, :].astype(F32)
        keys_ref[k * part : (k + 1) * part, :] = total.astype(BF16)
    for n in range(blocks // SPLIT):
        total = received_ref[n * SPLIT, part:, :].astype(F32)
        for k in range(1, SPLIT):
            total += received_ref[n * SPLIT + k, part:, :].astype(F32)
        lines_ref[n * strip : (n + 1) * strip, :] = total
    lines = dot(to_classes(rows, blocks // SPLIT), lines_ref[...].astype(BF16), 0, 0).astype(BF16)
    keys = dot(to_classes(rows, SPLIT), keys_ref[...], 0, 0).astype(BF16)
    query_ref[...] = lines[:, :width]
    attended_ref[...] = lines[:, width:]
    key_ref[...] = keys[:, :width]
    value_ref[...] = keys[:, width:]


def body(query_rows, key_rows, value_rows, out_grad, mix_pre, mix_post, block_order):
    blocks = lax.axis_size("seq")
    outer = lax.axis_size("row")
    owners = outer * lax.axis_size("col")
    rows, width = query_rows.shape
    heads = mix_pre.shape[0]
    scaling = DH ** (-0.5)
    strip = rows // blocks * SPLIT
    supers = blocks // SPLIT
    span = 2 * (supers + 1) * rows
    keys = supers * rows
    lines = blocks * strip
    slots = lines * HEADS
    whole = pl.BlockSpec(memory_space=pltpu.VMEM)
    table = pl.BlockSpec(memory_space=pltpu.SMEM)
    seq_shape = (blocks, rows // SPLIT + strip, 2 * width)
    head_shape = (owners, HEADS, (4 * supers + 1) * rows)
    static = dict(blocks=blocks, rows=rows, strip=strip)

    def call(kernel, ins, outs, scratch=(), dtype=BF16, **more):
        return pl.pallas_call(
            functools.partial(kernel, **static, **more),
            in_specs=ins,
            out_specs=[whole] * len(outs),
            out_shape=[jax.ShapeDtypeStruct(shape, dtype) for shape in outs],
            scratch_shapes=scratch,
            compiler_params=pltpu.CompilerParams(vmem_limit_bytes=VMEM_LIMIT),
            interpret=INTERP,
        )

    def exchange(values, axes):
        return near(lax.all_to_all(values, axes, split_axis=0, concat_axis=0, tiled=True))

    def near(values):
        return values if INTERP else pltpu.with_memory_space_constraint(values, pltpu.VMEM)

    def far(values):
        return values if INTERP else pltpu.with_memory_space_constraint(values, pltpu.HBM)

    (sent,) = call(
        send_kernel,
        [pl.BlockSpec(memory_space=pltpu.HBM)] * 4,
        [seq_shape],
        [pltpu.VMEM((rows, width), BF16)] * 4 + [pltpu.SemaphoreType.DMA((4,))],
        width=width,
    )(*[far(values) for values in (query_rows, key_rows, value_rows, out_grad)])
    received = exchange(sent, "seq")
    packed, key_value, line_rows = call(
        score_kernel,
        [table, whole],
        [head_shape, (keys, 2 * width), (slots, 2 * width)],
        [
            pltpu.SMEM((blocks,), jnp.int32),
            pltpu.VMEM((lines, 2 * width), F32),
            pltpu.VMEM((2, supers, HEADS * strip * SPLIT, rows), F32),
        ],
        width=width, scaling=scaling,
    )(block_order, received)
    weights, squashed, grads, sums = call(
        weigh_kernel,
        [whole] * 3,
        [(heads, span)] * 3 + [(SUMS, heads)],
        dtype=F32, heads=heads, outer=outer,
    )(exchange(packed, OWNER_AXES), mix_pre, mix_post)
    others = lax.ppermute(sums, "seq", [(s, s ^ 1) for s in range(blocks)])
    (mixed,) = call(
        mix_kernel,
        [whole] * 7,
        [head_shape],
        [pltpu.VMEM((2, heads, span), BF16)],
        heads=heads, outer=outer, scaling=scaling,
    )(near(weights), near(squashed), near(grads), sums, near(others), mix_pre, mix_post)
    (sent,) = call(
        grad_kernel,
        [table, whole, whole, whole],
        [seq_shape],
        [
            pltpu.VMEM((2, slots, keys), BF16),
            pltpu.VMEM((slots, width), F32),
            pltpu.SMEM((blocks,), jnp.int32),
        ],
        width=width,
    )(block_order, exchange(mixed, OWNER_AXES), near(key_value), near(line_rows))
    return call(
        final_kernel,
        [whole],
        [(rows, width)] * 4,
        [pltpu.VMEM((rows, 2 * width), BF16), pltpu.VMEM((rows, 2 * width), F32)],
        width=width,
    )(exchange(sent, "seq"))


def solution(mesh):
    spread = P("seq", HEAD_AXES)
    return jax.shard_map(
        body,
        mesh=mesh,
        in_specs=(spread, spread, spread, spread, P(), P(), P()),
        out_specs=(spread, spread, spread, spread),
        check_vma=False,
    )
```
